128 devices in a mesh: gx: 8 (over y, core), gy: 16 (over x, z).
Axes of the slice: x: 4, y: 4, z: 4, core: 2. Of those that a mesh axis runs over, the one named last changes fastest.
Arguments:
- log_perm: float32 [1, 32, 256, 4096], P(None, None, 'gx', 'gy'), may hold values from -4 to 4
- source: float32 [1, 32, 256, 4096], P(None, None, 'gx', 'gy'), may hold values from -24 to 24
Outputs:
- pressure: float32 [1, 32, 256, 4096], P(None, None, 'gx', 'gy')
- residual: float32 [1, 32, 256, 4096], P(None, None, 'gx', 'gy')
- flux_east: float32 [1, 32, 256, 4096], P(None, None, 'gx', 'gy')
- flux_north: float32 [1, 32, 256, 4096], P(None, None, 'gx', 'gy')
The draws below stay inside these ranges and needn't reach their ends.
All inputs are finite; a program needn't handle non-finite values.
Results may differ from the reference program's by a relative error of at most 0.0003.
Values sent between devices are 32-bit elements; how exact they have to be, the bound alone decides.
A program may use at most 128 MiB of HBM per device.

```python
import jax
import jax.numpy as jnp
from jax import lax

SAMPLES = 1
NZ = 32
OUTER = 2
NX = 256
NY = 4096


def levels(own_key, extent, shards, smallest, top_value):
    def one(dim, shards_of):
        heights = jax.random.uniform(jax.random.fold_in(jax.random.fold_in(own_key, 6), dim), (shards_of,), jnp.float32, smallest / len(shards), top_value / len(shards))
        return jnp.repeat(jnp.exp(heights), extent[dim] // shards_of).reshape((-1,) + (1,) * (len(extent) - dim - 1))

    loudness = one(*shards[0])
    for cut in shards[1:]:
        loudness = loudness * one(*cut)
    return loudness


def centred(key, extent, spread, bound, cuts=(), kind=jnp.bfloat16):
    loudness = levels(key, extent, cuts, -0.22, 0.18) if cuts else 1.0
    values = jax.random.normal(key, extent, jnp.float32) * spread * loudness
    return jnp.minimum(jnp.maximum(values, -bound), bound).astype(kind)


def setup_inputs(seed: int = 0) -> dict:
    key_list = jax.random.split(jax.random.key(seed), 3)
    return {
        "log_perm": centred(key_list[0], (SAMPLES, NZ, NX, NY), 1.0, 4.0, ((2, 8), (3, 16)), jnp.float32),
        "source": centred(key_list[1], (SAMPLES, NZ, NX, NY), 4.0, 24.0, ((2, 8), (3, 16)), jnp.float32),
    }


exact_mode = lax.Precision.HIGHEST


def harmonic(first_perm, second_perm):
    return 2.0 * first_perm * second_perm / (first_perm + second_perm)


def operator_terms(log_values):
    padded = jnp.exp(jnp.pad(log_values, ((0, 0), (1, 1), (1, 1))))
    trans_x = harmonic(padded[:, 1:, 1:-1], padded[:, :-1, 1:-1])
    trans_y = harmonic(padded[:, 1:-1, 1:], padded[:, 1:-1, :-1])
    interior = padded[:, 1:-1, 1:-1]
    trans_z = jnp.pad(harmonic(interior[1:], interior[:-1]), ((1, 1), (0, 0), (0, 0)))
    return trans_x, trans_y, trans_z


def apply_operator(field_in, transmit):
    trans_x, trans_y, trans_z = transmit
    padded = jnp.pad(field_in, ((0, 0), (1, 1), (1, 1)))
    vertical = jnp.pad(field_in, ((1, 1), (0, 0), (0, 0)))
    result = trans_x[:, 1:] * (field_in - padded[:, 2:, 1:-1]) + trans_x[:, :-1] * (field_in - padded[:, :-2, 1:-1])
    result = result + trans_y[:, :, 1:] * (field_in - padded[:, 1:-1, 2:]) + trans_y[:, :, :-1] * (field_in - padded[:, 1:-1, :-2])
    result = result + trans_z[1:] * (field_in - vertical[2:]) + trans_z[:-1] * (field_in - vertical[:-2])
    return result


def recurrence(gram_matrix):
    batch_count = gram_matrix.shape[0]
    identity = jnp.eye(5, dtype=jnp.float32)
    direc_coef = jnp.broadcast_to(identity[0], (batch_count, 5))
    resid_coef = jnp.broadcast_to(identity[3], (batch_count, 5))
    sol_coef = jnp.zeros((batch_count, 5), jnp.float32)
    zero_col = jnp.zeros((batch_count,), jnp.float32)

    def shifted(coef_in):
        return jnp.stack([zero_col, coef_in[:, 0], coef_in[:, 1], zero_col, coef_in[:, 3]], axis=1)

    def quadratic(left_coef, right_coef):
        return jnp.einsum("si,sij,sj->s", left_coef, gram_matrix, right_coef, precision=exact_mode)

    for inner_turn in range(2):
        images = shifted(direc_coef)
        rho_old = quadratic(resid_coef, resid_coef)
        step_size = (rho_old / quadratic(direc_coef, images))[:, None]
        sol_coef = sol_coef + step_size * direc_coef
        resid_coef = resid_coef - step_size * images
        ratio_new = (quadratic(resid_coef, resid_coef) / rho_old)[:, None]
        direc_coef = resid_coef + ratio_new * direc_coef
    return sol_coef, resid_coef, direc_coef


def one_sample(sample_pair):
    log_values, source_field = sample_pair
    transmit = operator_terms(log_values)
    pressure = jnp.zeros_like(source_field)
    resid_field = source_field
    direc_field = source_field
    for outer_turn in range(OUTER):
        power_one = apply_operator(direc_field, transmit)
        power_two = apply_operator(power_one, transmit)
        resid_image = apply_operator(resid_field, transmit)
        basis = jnp.stack([direc_field, power_one, power_two, resid_field, resid_image])
        gram_matrix = jnp.einsum("izxy,jzxy->ij", basis, basis, precision=exact_mode)
        sol_coef, resid_coef, direc_coef = recurrence(gram_matrix[None])
        pressure = pressure + jnp.einsum("i,izxy->zxy", sol_coef[0], basis, precision=exact_mode)
        resid_field = jnp.einsum("i,izxy->zxy", resid_coef[0], basis, precision=exact_mode)
        direc_field = jnp.einsum("i,izxy->zxy", direc_coef[0], basis, precision=exact_mode)
    residual = source_field - apply_operator(pressure, transmit)
    padded = jnp.pad(pressure, ((0, 0), (1, 1), (1, 1)))
    flux_east = transmit[0][:, 1:] * (pressure - padded[:, 2:, 1:-1])
    flux_north = transmit[1][:, :, 1:] * (pressure - padded[:, 1:-1, 2:])
    return pressure, residual, flux_east, flux_north


def reference(log_perm, source):
    pressure, residual, flux_east, flux_north = lax.map(one_sample, (log_perm, source))
    return (pressure, residual, flux_east, flux_north)
```

```python
import functools

import jax
import jax.numpy as jnp
from jax import lax
from jax.experimental import pallas as pl
from jax.experimental.pallas import tpu as pltpu
from jax.sharding import PartitionSpec as P

MESH = pl.DeviceIdType.MESH
F32 = jnp.float32
TOP = 8
ROWS = 48
WIDE = (4, 12, 20, 28, 36)
OWN = (8, 16, 24, 32)
DIRS = ((0, 1), (0, -1), (1, 0), (-1, 0), (1, 1), (1, -1), (-1, 1), (-1, -1))


def iota(dim):
    return lax.broadcasted_iota(jnp.int32, (8, 128), dim)


def roll(value, amount):
    return pltpu.roll(value, amount % 128 if isinstance(amount, int) else amount, 1)


def two_sum(a, b):
    s = a + b
    t = s - a
    return s, (a - (s - t)) + (b - t)


def quick(a, b):
    s = a + b
    return s, b - (s - a)


def pair_add(x, y):
    s, e = two_sum(x[0], y[0])
    return quick(s, e + (x[1] + y[1]))


def halves(a):
    t = a * 4097.0
    hi = t - (t - a)
    return hi, a - hi


def pair_mul(x, y):
    p = x[0] * y[0]
    xh, xl = halves(x[0])
    yh, yl = halves(y[0])
    e = ((xh * yh - p) + xh * yl + xl * yh) + xl * yl
    return quick(p, e + (x[0] * y[1] + x[1] * y[0]))


def neg(x):
    return (-x[0], -x[1])


def pair_div(x, y):
    q = x[0] / y[0]
    zero = jnp.zeros_like(q)
    rest = pair_add(x, neg(pair_mul(y, (q, zero))))
    return quick(q, rest[0] / y[0])


def coefficients(moments):
    resid, direc = dict(enumerate(moments)), dict(enumerate(moments))
    steps, ratios = [], []
    for k in range(4):
        step = pair_div(resid[k], direc[k + 1])
        steps.append(step)
        if k == 3:
            break
        fresh = {}
        for l in range(k + 1, 7 - k):
            fresh[l] = pair_add(resid[l], neg(pair_mul(step, direc[l + 1])))
        ratio = neg(pair_div(pair_mul(step, fresh[k + 1]), resid[k]))
        ratios.append(ratio)
        direc = {l: pair_add(fresh[l], pair_mul(ratio, direc[l])) for l in fresh}
        resid = fresh
    a = [s[0] for s in steps]
    b = [r[0] for r in ratios]
    one = jnp.ones_like(a[0])
    r, p = [one], [one]
    x = [a[0]]
    for k in range(3):
        moved = [None] + [a[k] * c for c in p]
        r = [
            moved[m] * -1.0 if m >= len(r) else (r[m] if moved[m] is None else r[m] - moved[m])
            for m in range(len(moved))
        ]
        p = [r[m] + b[k] * p[m] if m < len(p) else r[m] for m in range(len(r))]
        x = [x[m] + a[k + 1] * p[m] if m < len(x) else a[k + 1] * p[m] for m in range(len(p))]
    return x


def tree(hi, lo):
    for shift in (4, 2, 1):
        hi, lo = pair_add((hi, lo), (pltpu.roll(hi, shift, 0), pltpu.roll(lo, shift, 0)))
    return hi, lo


def build(nz, gx, gy, lp_ref, src_ref, v0, v1, v2, v3, v4, tx, ty, q, coef,
          lp, w, tz, s_own, s_left, s_right, ws, txs, tys, tzs, b0, b1, b2, b3, fzs,
          send_row, red_a, red_b, load_sem, x_send, x_recv, s_send, s_recv, a_send, a_recv, c_send, c_recv):
    i = lax.axis_index("gx")
    j = lax.axis_index("gy")
    zp_count = nz // 8
    fields = (v0, v1, v2, v3, v4)
    strips = (b0, b1, b2, b3)
    lane, sub = iota(1), iota(0)
    l16 = lane % 16

    barrier = pltpu.get_barrier_semaphore()
    for d in range(1, gx):
        pl.semaphore_signal(barrier, inc=1, device_id=(lax.rem(i + d, gx), j), device_id_type=MESH)
    for d in range(1, gy):
        pl.semaphore_signal(barrier, inc=1, device_id=(i, lax.rem(j + d, gy)), device_id_type=MESH)

    def inside(di, dj):
        ok = None
        for cond in (
            [] if di == 0 else [i < gx - 1] if di > 0 else [i > 0]
        ) + ([] if dj == 0 else [j < gy - 1] if dj > 0 else [j > 0]):
            ok = cond if ok is None else jnp.logical_and(ok, cond)
        return ok

    for di, dj in DIRS[4:]:
        @pl.when(inside(di, dj))
        def _():
            pl.semaphore_signal(barrier, inc=1, device_id=(i + di, j + dj), device_id_type=MESH)

    loads = []
    for n, (source, target) in enumerate(((src_ref, v0), (lp_ref, lp))):
        for h in range(2):
            copy = pltpu.make_async_copy(
                source.at[0, :, :, pl.ds(128 * h, 128)],
                target.at[h, :, pl.ds(TOP, 32), :],
                load_sem.at[2 * n + h],
            )
            copy.start()
            loads.append(copy)

    zero4 = jnp.zeros((4, 128), F32)

    @pl.when(i == 0)
    def _():
        def fill(z, carry):
            for h in range(2):
                v0[h, z, 4:8] = zero4
                lp[h, z, 4:8] = zero4
            return carry
        lax.fori_loop(0, nz, fill, 0)
        for zp in range(zp_count):
            for buf in (s_own, s_left, s_right):
                buf[zp, 4:8] = zero4

    @pl.when(i == gx - 1)
    def _():
        def fill(z, carry):
            for h in range(2):
                v0[h, z, 40:44] = zero4
                lp[h, z, 40:44] = zero4
            return carry
        lax.fori_loop(0, nz, fill, 0)
        for zp in range(zp_count):
            for buf in (s_own, s_left, s_right):
                buf[zp, 40:44] = zero4

    for edge, buf in ((j == 0, s_left), (j == gy - 1, s_right)):
        @pl.when(edge)
        def _():
            for zp in range(zp_count):
                buf[zp, 4:8] = zero4
                buf[zp, 40:44] = zero4
                for r in OWN:
                    buf[zp, r:r + 8] = jnp.zeros((8, 128), F32)

    for n, red in ((gx, red_a), (gy, red_b)):
        for r in range(n, red.shape[0]):
            red[r:r + 1, :] = jnp.zeros((1, 128), F32)

    inner_i = (i > 0).astype(jnp.int32) + (i < gx - 1).astype(jnp.int32)
    inner_j = (j > 0).astype(jnp.int32) + (j < gy - 1).astype(jnp.int32)
    pl.semaphore_wait(barrier, gx - 1 + gy - 1 + inner_i * inner_j)

    x_copies = []
    for step, first, land in ((1, 28, 4), (-1, 0, 40)):
        group = []
        for n, (source, target) in enumerate(((lp_ref, lp), (src_ref, v0))):
            for h in range(2):
                slot = (0 if step > 0 else 4) + 2 * n + h
                group.append(pltpu.make_async_remote_copy(
                    src_ref=source.at[0, :, pl.ds(first, 4), pl.ds(128 * h, 128)],
                    dst_ref=target.at[h, :, pl.ds(land, 4), :],
                    send_sem=x_send.at[slot],
                    recv_sem=x_recv.at[slot],
                    device_id=(i + step, j),
                    device_id_type=MESH,
                ))
        x_copies.append((step, group))

        @pl.when(inside(step, 0))
        def _():
            for copy in group:
                copy.start()

    for copy in loads:
        copy.wait()

    def pack(zp, carry):
        for r in OWN:
            packed = jnp.zeros((8, 128), F32)
            for g in range(8):
                z = g * zp_count + zp
                fld = jnp.where(lane < 64, v0[0, z, r:r + 8], v0[1, z, r:r + 8])
                log = jnp.where(lane < 64, lp[0, z, r:r + 8], lp[1, z, r:r + 8])
                both = jnp.where(l16 < 8, roll(log, 16 * g + 4), roll(fld, 16 * g + 12))
                packed = jnp.where(lane // 16 == g, both, packed)
            s_own[zp, r:r + 8] = packed
        return carry

    lax.fori_loop(0, zp_count, pack, 0)

    s_copies = []
    for n, (di, dj) in enumerate(DIRS):
        target = s_own if dj == 0 else s_left if dj > 0 else s_right
        if di == 0:
            first, land, count = 8, 8, 32
        elif di > 0:
            first, land, count = 36, 4, 4
        else:
            first, land, count = 8, 40, 4
        copy = pltpu.make_async_remote_copy(
            src_ref=s_own.at[:, pl.ds(first, count), :],
            dst_ref=target.at[:, pl.ds(land, count), :],
            send_sem=s_send.at[n],
            recv_sem=s_recv.at[n],
            device_id=(i + di, j + dj),
            device_id_type=MESH,
        )
        s_copies.append((di, dj, copy))

    for di, dj, copy in s_copies[4:] + s_copies[:4]:
        @pl.when(inside(di, dj))
        def _():
            copy.start()

    def invert(z, carry):
        for h in range(2):
            for r in OWN:
                w[h, z, r:r + 8] = jnp.exp(-lp[h, z, r:r + 8])
        return carry

    lax.fori_loop(0, nz, invert, 0)

    def faces(z, carry):
        above = jnp.minimum(z + 1, nz - 1)
        top = jnp.where(z < nz - 1, 2.0, 0.0)
        for r in OWN:
            w0, w1 = w[0, z, r:r + 8], w[1, z, r:r + 8]
            n0, n1 = roll(w0, -1), roll(w1, -1)
            ty[0, z, r:r + 8] = 2.0 / (w0 + jnp.where(lane == 127, n1, n0))
            ty[1, z, r:r + 8] = 2.0 / (w1 + n1)
            for h, mid in ((0, w0), (1, w1)):
                tx[h, z, r:r + 8] = 2.0 / (mid + w[h, z, r + 1:r + 9])
                tz[h, z, r:r + 8] = top / (mid + w[h, above, r:r + 8])
        return carry

    lax.fori_loop(0, nz, faces, 0)

    for di, dj, copy in s_copies:
        @pl.when(inside(-di, -dj))
        def _():
            copy.wait_recv()

    for zp in range(zp_count):
        for r in WIDE:
            own, left, right = (s[zp, r:r + 8] for s in (s_own, s_left, s_right))
            moved = roll(jnp.where(l16 < 12, left, own), -8)
            b0[zp, r:r + 8] = jnp.where(l16 < 8, moved, jnp.where(l16 < 12, own, right))
            moved = roll(jnp.where(l16 < 4, own, right), 8)
            log = jnp.where(l16 < 8, jnp.where(l16 < 4, left, own), moved)
            ws[zp, r:r + 8] = jnp.exp(-log)
    for zp in range(zp_count):
        for r in WIDE:
            mid = ws[zp, r:r + 8]
            txs[zp, r:r + 8] = 2.0 / (mid + ws[zp, r + 1:r + 9])
            tys[zp, r:r + 8] = 2.0 / (mid + roll(mid, -1))
            if zp < zp_count - 1:
                tzs[zp, r:r + 8] = 2.0 / (mid + ws[zp + 1, r:r + 8])
            else:
                tzs[zp, r:r + 8] = jnp.where(lane < 112, 2.0 / (mid + roll(ws[0, r:r + 8], -16)), 0.0)
    keep_cols = jnp.logical_and(jnp.logical_or(l16 >= 4, j > 0), jnp.logical_or(l16 < 12, j < gy - 1))
    keep_top = jnp.logical_or(sub >= 4, i > 0)
    keep_bottom = jnp.logical_or(sub < 4, i < gx - 1)
    for k in range(4):
        field = strips[k]
        if k < 3:
            for zp in range(zp_count):
                for r in WIDE:
                    mid = field[zp, r:r + 8]
                    above = field[zp + 1, r:r + 8] if zp < zp_count - 1 else roll(field[0, r:r + 8], -16)
                    fzs[zp, r:r + 8] = tzs[zp, r:r + 8] * (mid - above)
        for zp in range(zp_count):
            for r in WIDE:
                mid = field[zp, r:r + 8]
                fy = tys[zp, r:r + 8] * (mid - roll(mid, -1))
                q[k, zp, r:r + 8] = jnp.where(l16 == 8, roll(fy, 5), roll(fy, -4))
                if k == 3:
                    continue
                below = fzs[zp - 1, r:r + 8] if zp else roll(fzs[zp_count - 1, r:r + 8], 16)
                total = txs[zp, r:r + 8] * (mid - field[zp, r + 1:r + 9])
                total = total + txs[zp, r - 1:r + 7] * (mid - field[zp, r - 1:r + 7])
                total = total + (fy - roll(fy, 1)) + (fzs[zp, r:r + 8] - below)
                keep = keep_cols
                if r == 4:
                    keep = jnp.logical_and(keep, keep_top)
                if r == 36:
                    keep = jnp.logical_and(keep, keep_bottom)
                strips[k + 1][zp, r:r + 8] = jnp.where(keep, total, 0.0)

    for step, group in x_copies:
        @pl.when(inside(-step, 0))
        def _():
            for copy in group:
                copy.wait_recv()

    def invert_rim(z, carry):
        for h in range(2):
            both = jnp.exp(-jnp.where(sub < 4, lp[h, z, 4:12], lp[h, z, 36:44]))
            w[h, z, 4:8] = both[0:4]
            w[h, z, 40:44] = both[4:8]
        return carry

    lax.fori_loop(0, nz, invert_rim, 0)

    def faces_rim(z, carry):
        above = jnp.minimum(z + 1, nz - 1)
        top = jnp.where(z < nz - 1, 2.0, 0.0)
        mids = [jnp.where(sub < 4, w[h, z, 4:12], w[h, z, 35:43]) for h in range(2)]
        moved = [roll(m, -1) for m in mids]
        moved[0] = jnp.where(lane == 127, moved[1], moved[0])
        for h in range(2):
            across = jnp.where(sub < 4, w[h, z, 5:13], w[h, z, 36:44])
            higher = jnp.where(sub < 4, w[h, above, 4:12], w[h, above, 35:43])
            for ref, value in (
                (tx, 2.0 / (mids[h] + across)),
                (ty, 2.0 / (mids[h] + moved[h])),
                (tz, top / (mids[h] + higher)),
            ):
                ref[h, z, 4:8] = value[0:4]
                ref[h, z, 39:43] = value[4:8]
        return carry

    lax.fori_loop(0, nz, faces_rim, 0)

    moments = []
    for k in range(4):
        src, dst = fields[k], fields[k + 1]
        tiles = WIDE if k < 3 else OWN

        def layer(z, carry, k=k, src=src, dst=dst, tiles=tiles):
            sums, below = carry
            above = jnp.minimum(z + 1, nz - 1)
            turn = lax.rem(120 - 16 * (z // zp_count) + 128, 128)
            sums, below, after = list(sums), list(below), []
            for n, r in enumerate(tiles):
                rows = slice(r, r + 8)
                up, down = slice(r + 1, r + 9), slice(r - 1, r + 7)
                side = roll(q[k, lax.rem(z, zp_count), rows], turn)
                v = [src[h, z, rows] for h in range(2)]
                moved = [roll(v[h], -1) for h in range(2)]
                moved[0] = jnp.where(lane == 127, moved[1], moved[0])
                fy = [ty[h, z, rows] * (v[h] - moved[h]) for h in range(2)]
                fy[1] = jnp.where(lane == 127, side, fy[1])
                back = [roll(fy[h], 1) for h in range(2)]
                back[1] = jnp.where(lane == 0, back[0], back[1])
                back[0] = jnp.where(lane == 0, side, back[0])
                for h in range(2):
                    fz = tz[h, z, rows] * (v[h] - src[h, above, rows])
                    total = tx[h, z, rows] * (v[h] - src[h, z, up])
                    total = total + tx[h, z, down] * (v[h] - src[h, z, down])
                    total = total + (fy[h] - back[h]) + (fz - below[2 * n + h])
                    after.append(fz)
                    mine, new = v[h], total
                    if r == 4:
                        total = jnp.where(keep_top, total, 0.0)
                        mine = jnp.where(sub >= 4, mine, 0.0)
                        new = jnp.where(sub >= 4, total, 0.0)
                    if r == 36:
                        total = jnp.where(keep_bottom, total, 0.0)
                        mine = jnp.where(sub < 4, mine, 0.0)
                        new = jnp.where(sub < 4, total, 0.0)
                    dst[h, z, rows] = total
                    if k == 0:
                        sums[2] = sums[2] + mine * mine
                    sums[0] = sums[0] + mine * new
                    if k < 3:
                        sums[1] = sums[1] + new * new
            return tuple(sums), tuple(after)

        zero = jnp.zeros((8, 128), F32)
        count = 3 if k == 0 else 2 if k < 3 else 1
        sums, _ = lax.fori_loop(0, nz, layer, ((zero,) * count, (zero,) * (2 * len(tiles))))
        if k == 0:
            moments.append(sums[2])
        moments.extend(sums[:2])

    row = jnp.zeros((8, 128), F32)
    for n, part in enumerate(moments):
        row = jnp.where(lane == n, jnp.sum(part, axis=1, keepdims=True), row)
    row = jnp.sum(row, axis=0, keepdims=True)

    def exchange(value, slot, red, count, send, recv, where):
        send_row[slot:slot + 1, :] = value
        red[0:1, :] = value
        copies = []
        for d in range(1, count):
            copies.append(pltpu.make_async_remote_copy(
                src_ref=send_row.at[pl.ds(slot, 1), :],
                dst_ref=red.at[pl.ds(count - d, 1), :],
                send_sem=send.at[d],
                recv_sem=recv.at[count - d],
                device_id=where(d),
                device_id_type=MESH,
            ))
        for copy in copies:
            copy.start()
        for copy in copies:
            copy.wait_recv()
        return copies

    sent = exchange(row, 0, red_a, gx, a_send, a_recv, lambda d: (lax.rem(i + d, gx), j))
    part = red_a[...]
    hi, lo = tree(part, jnp.zeros_like(part))
    row = jnp.where(lane < 8, hi, pltpu.roll(lo, 8, 1))[0:1]
    sent += exchange(row, 8, red_b, gy, c_send, c_recv, lambda d: (i, lax.rem(j + d, gy)))
    parts = []
    for r in range(0, red_b.shape[0], 8):
        part = red_b[r:r + 8]
        parts.append((part, pltpu.roll(part, 120, 1)))
    total = parts[0]
    for part in parts[1:]:
        total = pair_add(total, part)
    hi, lo = tree(*total)
    splat = [
        (jnp.broadcast_to(hi[:, n:n + 1], (8, 128)), jnp.broadcast_to(lo[:, n:n + 1], (8, 128)))
        for n in range(8)
    ]
    for n, value in enumerate(coefficients(splat)):
        coef[n] = value

    for copy in sent:
        copy.wait_send()
    for di, dj, copy in s_copies:
        @pl.when(inside(di, dj))
        def _():
            copy.wait_send()
    for step, group in x_copies:
        @pl.when(inside(step, 0))
        def _():
            for copy in group:
                copy.wait_send()


def finish(nz, v0, v1, v2, v3, v4, tx, ty, q, coef, p_out, r_out, e_out, n_out,
           p_buf, r_buf, e_buf, n_buf, wide, side, sems):
    zp_count = nz // 8
    chunk = nz // 4
    lane = iota(1)
    c = [coef[n] for n in range(4)]

    def combine(parts):
        return (c[0] * parts[0] + c[1] * parts[1]) + (c[2] * parts[2] + c[3] * parts[3])

    for zp in range(zp_count):
        for r in OWN:
            side[zp, r:r + 8] = combine([q[k, zp, r:r + 8] for k in range(4)])

    def layer(z, carry):
        turn = lax.rem(120 - 16 * (z // zp_count) + 128, 128)
        press = {}
        for r in OWN:
            for h in range(2):
                v = [f[h, z, r:r + 8] for f in (v0, v1, v2, v3)]
                press[h, r] = combine(v)
                wide[h, r:r + 8] = press[h, r]
                cols = slice(128 * h, 128 * h + 128)
                p_buf[z, r - 8:r, cols] = press[h, r]
                r_buf[z, r - 8:r, cols] = v[0] - combine(v[1:] + [v4[h, z, r:r + 8]])
        for h in range(2):
            wide[h, 40:48] = combine([f[h, z, 40:48] for f in (v0, v1, v2, v3)])
        for r in OWN:
            moved = [roll(press[h, r], -1) for h in range(2)]
            moved[0] = jnp.where(lane == 127, moved[1], moved[0])
            for h in range(2):
                cols = slice(128 * h, 128 * h + 128)
                e_buf[z, r - 8:r, cols] = tx[h, z, r:r + 8] * (press[h, r] - wide[h, r + 1:r + 9])
                north = ty[h, z, r:r + 8] * (press[h, r] - moved[h])
                if h == 1:
                    north = jnp.where(lane == 127, roll(side[lax.rem(z, zp_count), r:r + 8], turn), north)
                n_buf[z, r - 8:r, cols] = north
        return carry

    copies = []
    for part in range(4):
        lax.fori_loop(part * chunk, (part + 1) * chunk, layer, 0)
        for n, (buf, out) in enumerate(((p_buf, p_out), (r_buf, r_out), (e_buf, e_out), (n_buf, n_out))):
            copy = pltpu.make_async_copy(
                buf.at[pl.ds(part * chunk, chunk)],
                out.at[0, pl.ds(part * chunk, chunk)],
                sems.at[4 * part + n],
            )
            copy.start()
            copies.append(copy)
    for copy in copies:
        copy.wait()


def solution(mesh):
    gx, gy = mesh.shape["gx"], mesh.shape["gy"]

    def on_device(log_perm, source):
        nz = log_perm.shape[1]
        zp = nz // 8
        field = (2, nz, ROWS, 128)
        strip = (zp, ROWS, 128)
        vmem = pl.BlockSpec(memory_space=pltpu.VMEM)
        hbm = pl.BlockSpec(memory_space=pltpu.HBM)
        made = pl.pallas_call(
            functools.partial(build, nz, gx, gy),
            out_shape=[pltpu.VMEM(field, F32)] * 7 + [pltpu.VMEM((4,) + strip, F32), pltpu.VMEM((4, 8, 128), F32)],
            in_specs=[hbm] * 2,
            out_specs=[vmem] * 9,
            scratch_shapes=[pltpu.VMEM(field, F32)] * 3
            + [pltpu.VMEM(strip, F32)] * 12
            + [
                pltpu.VMEM((16, 128), F32),
                pltpu.VMEM((8, 128), F32),
                pltpu.VMEM((max(8, gy), 128), F32),
                pltpu.SemaphoreType.DMA((4,)),
                pltpu.SemaphoreType.DMA((8,)),
                pltpu.SemaphoreType.DMA((8,)),
                pltpu.SemaphoreType.DMA((8,)),
                pltpu.SemaphoreType.DMA((8,)),
                pltpu.SemaphoreType.DMA((gx,)),
                pltpu.SemaphoreType.DMA((gx,)),
                pltpu.SemaphoreType.DMA((gy,)),
                pltpu.SemaphoreType.DMA((gy,)),
            ],
            compiler_params=pltpu.CompilerParams(
                collective_id=0, has_side_effects=True, vmem_limit_bytes=24 << 20
            ),
            name="build",
        )(*(pltpu.with_memory_space_constraint(x, pltpu.HBM) for x in (log_perm, source)))
        shape = jax.ShapeDtypeStruct(log_perm.shape, F32)
        return pl.pallas_call(
            functools.partial(finish, nz),
            out_shape=[shape] * 4,
            in_specs=[vmem] * 9,
            out_specs=[hbm] * 4,
            scratch_shapes=[pltpu.VMEM((nz, 32, 256), F32)] * 4
            + [pltpu.VMEM((2, ROWS, 128), F32), pltpu.VMEM(strip, F32), pltpu.SemaphoreType.DMA((16,))],
            compiler_params=pltpu.CompilerParams(vmem_limit_bytes=24 << 20),
            name="finish",
        )(*made)

    spec = P(None, None, "gx", "gy")
    return jax.shard_map(
        on_device, mesh=mesh, in_specs=(spec, spec), out_specs=(spec,) * 4, check_vma=False
    )
```

```python
import functools

import jax
import jax.numpy as jnp
from jax import lax
from jax.experimental import pallas as pl
from jax.experimental.pallas import tpu as pltpu
from jax.sharding import PartitionSpec as P

MESH = pl.DeviceIdType.MESH
F32 = jnp.float32
TOP = 8
ROWS = 48
WIDE = (4, 12, 20, 28, 36)
OWN = (8, 16, 24, 32)
PARTS = 4
BLOCK = 4
DIRS = ((0, 1), (0, -1), (1, 0), (-1, 0), (1, 1), (1, -1), (-1, 1), (-1, -1))


def iota(dim):
    return lax.broadcasted_iota(jnp.int32, (8, 128), dim)


def roll(value, amount):
    return pltpu.roll(value, amount % 128 if isinstance(amount, int) else amount, 1)


def two_sum(a, b):
    s = a + b
    t = s - a
    return s, (a - (s - t)) + (b - t)


def quick(a, b):
    s = a + b
    return s, b - (s - a)


def pair_add(x, y):
    s, e = two_sum(x[0], y[0])
    return quick(s, e + (x[1] + y[1]))


def halves(a):
    t = a * 4097.0
    hi = t - (t - a)
    return hi, a - hi


def pair_mul(x, y):
    p = x[0] * y[0]
    xh, xl = halves(x[0])
    yh, yl = halves(y[0])
    e = ((xh * yh - p) + xh * yl + xl * yh) + xl * yl
    return quick(p, e + (x[0] * y[1] + x[1] * y[0]))


def neg(x):
    return (-x[0], -x[1])


def pair_div(x, y):
    q = x[0] / y[0]
    zero = jnp.zeros_like(q)
    rest = pair_add(x, neg(pair_mul(y, (q, zero))))
    return quick(q, rest[0] / y[0])


def coefficients(moments):
    resid, direc = dict(enumerate(moments)), dict(enumerate(moments))
    steps, ratios = [], []
    for k in range(4):
        step = pair_div(resid[k], direc[k + 1])
        steps.append(step)
        if k == 3:
            break
        fresh = {}
        for l in range(k + 1, 7 - k):
            fresh[l] = pair_add(resid[l], neg(pair_mul(step, direc[l + 1])))
        ratio = neg(pair_div(pair_mul(step, fresh[k + 1]), resid[k]))
        ratios.append(ratio)
        direc = {l: pair_add(fresh[l], pair_mul(ratio, direc[l])) for l in fresh}
        resid = fresh
    a = [s[0] for s in steps]
    b = [r[0] for r in ratios]
    one = jnp.ones_like(a[0])
    r, p = [one], [one]
    x = [a[0]]
    for k in range(3):
        moved = [None] + [a[k] * c for c in p]
        r = [
            moved[m] * -1.0 if m >= len(r) else (r[m] if moved[m] is None else r[m] - moved[m])
            for m in range(len(moved))
        ]
        p = [r[m] + b[k] * p[m] if m < len(p) else r[m] for m in range(len(r))]
        x = [x[m] + a[k + 1] * p[m] if m < len(x) else a[k + 1] * p[m] for m in range(len(p))]
    return x


def shifted(pair):
    lane = iota(1)
    right = [roll(p, -1) for p in pair]
    left = [roll(p, 1) for p in pair]
    right[0] = jnp.where(lane == 127, right[1], right[0])
    left[1] = jnp.where(lane == 0, left[0], left[1])
    return right, left


def tree(hi, lo):
    for shift in (4, 2, 1):
        hi, lo = pair_add((hi, lo), (pltpu.roll(hi, shift, 0), pltpu.roll(lo, shift, 0)))
    return hi, lo


def gather(nz, gx, gy, lp_ref, src_ref, v0, tx, ty, tz, tym, yp, ym, q,
           lp, w, s_own, s_left, s_right, ws, txs, tys, tzs, b0, b1, b2, b3, fzs,
           load_sem, x_send, x_recv, s_send, s_recv):
    i = lax.axis_index("gx")
    j = lax.axis_index("gy")
    zp_count = nz // 8
    strips = (b0, b1, b2, b3)
    lane, sub = iota(1), iota(0)
    l16 = lane % 16

    def inside(di, dj):
        ok = None
        for cond in (
            [] if di == 0 else [i < gx - 1] if di > 0 else [i > 0]
        ) + ([] if dj == 0 else [j < gy - 1] if dj > 0 else [j > 0]):
            ok = cond if ok is None else jnp.logical_and(ok, cond)
        return ok

    barrier = pltpu.get_barrier_semaphore()
    for di, dj in DIRS:
        @pl.when(inside(di, dj))
        def _():
            pl.semaphore_signal(barrier, inc=1, device_id=(i + di, j + dj), device_id_type=MESH)

    loads = []
    for n, (source, target) in enumerate(((src_ref, v0), (lp_ref, lp))):
        for h in range(2):
            copy = pltpu.make_async_copy(
                source.at[0, :, :, pl.ds(128 * h, 128)],
                target.at[h, :, pl.ds(TOP, 32), :],
                load_sem.at[2 * n + h],
            )
            copy.start()
            loads.append(copy)

    zero4 = jnp.zeros((4, 128), F32)

    @pl.when(i == 0)
    def _():
        def fill(z, carry):
            for h in range(2):
                v0[h, z, 4:8] = zero4
                lp[h, z, 4:8] = zero4
            return carry
        lax.fori_loop(0, nz, fill, 0)
        for zp in range(zp_count):
            for buf in (s_own, s_left, s_right):
                buf[zp, 4:8] = zero4

    @pl.when(i == gx - 1)
    def _():
        def fill(z, carry):
            for h in range(2):
                v0[h, z, 40:44] = zero4
                lp[h, z, 40:44] = zero4
            return carry
        lax.fori_loop(0, nz, fill, 0)
        for zp in range(zp_count):
            for buf in (s_own, s_left, s_right):
                buf[zp, 40:44] = zero4

    for edge, buf in ((j == 0, s_left), (j == gy - 1, s_right)):
        @pl.when(edge)
        def _():
            for zp in range(zp_count):
                buf[zp, 4:8] = zero4
                buf[zp, 40:44] = zero4
                for r in OWN:
                    buf[zp, r:r + 8] = jnp.zeros((8, 128), F32)

    inner_i = (i > 0).astype(jnp.int32) + (i < gx - 1).astype(jnp.int32)
    inner_j = (j > 0).astype(jnp.int32) + (j < gy - 1).astype(jnp.int32)
    pl.semaphore_wait(barrier, inner_i + inner_j + inner_i * inner_j)

    x_copies = []
    for step, first, land in ((1, 28, 4), (-1, 0, 40)):
        group = []
        for n, (source, target) in enumerate(((lp_ref, lp), (src_ref, v0))):
            for h in range(2):
                slot = (0 if step > 0 else 4) + 2 * n + h
                group.append(pltpu.make_async_remote_copy(
                    src_ref=source.at[0, :, pl.ds(first, 4), pl.ds(128 * h, 128)],
                    dst_ref=target.at[h, :, pl.ds(land, 4), :],
                    send_sem=x_send.at[slot],
                    recv_sem=x_recv.at[slot],
                    device_id=(i + step, j),
                    device_id_type=MESH,
                ))
        x_copies.append((step, group))

        @pl.when(inside(step, 0))
        def _():
            for copy in group:
                copy.start()

    for copy in loads:
        copy.wait()

    def pack(zp, carry):
        for r in OWN:
            packed = jnp.zeros((8, 128), F32)
            for g in range(8):
                z = g * zp_count + zp
                fld = jnp.where(lane < 64, v0[0, z, r:r + 8], v0[1, z, r:r + 8])
                log = jnp.where(lane < 64, lp[0, z, r:r + 8], lp[1, z, r:r + 8])
                both = jnp.where(l16 < 8, roll(log, 16 * g + 4), roll(fld, 16 * g + 12))
                packed = jnp.where(lane // 16 == g, both, packed)
            s_own[zp, r:r + 8] = packed
        return carry

    lax.fori_loop(0, zp_count, pack, 0)

    s_copies = []
    for n, (di, dj) in enumerate(DIRS):
        target = s_own if dj == 0 else s_left if dj > 0 else s_right
        if di == 0:
            first, land, count = 8, 8, 32
        elif di > 0:
            first, land, count = 36, 4, 4
        else:
            first, land, count = 8, 40, 4
        copy = pltpu.make_async_remote_copy(
            src_ref=s_own.at[:, pl.ds(first, count), :],
            dst_ref=target.at[:, pl.ds(land, count), :],
            send_sem=s_send.at[n],
            recv_sem=s_recv.at[n],
            device_id=(i + di, j + dj),
            device_id_type=MESH,
        )
        s_copies.append((di, dj, copy))

    for di, dj, copy in s_copies[4:] + s_copies[:4]:
        @pl.when(inside(di, dj))
        def _():
            copy.start()

    def invert(z, carry):
        for h in range(2):
            for r in OWN:
                w[h, z, r:r + 8] = jnp.exp(-lp[h, z, r:r + 8])
        return carry

    lax.fori_loop(0, nz, invert, 0)

    def faces(z, carry):
        above = jnp.minimum(z + 1, nz - 1)
        top = jnp.where(z < nz - 1, 2.0, 0.0)
        for r in OWN:
            mids = [w[h, z, r:r + 8] for h in range(2)]
            right, left = shifted(mids)
            more, less = shifted([v0[h, z, r:r + 8] for h in range(2)])
            for h, mid in enumerate(mids):
                ty[h, z, r:r + 8] = 2.0 / (mid + right[h])
                tym[h, z, r:r + 8] = 2.0 / (mid + left[h])
                tx[h, z, r:r + 8] = 2.0 / (mid + w[h, z, r + 1:r + 9])
                tz[h, z, r:r + 8] = top / (mid + w[h, above, r:r + 8])
                yp[h, z, r:r + 8] = more[h]
                ym[h, z, r:r + 8] = less[h]
        return carry

    lax.fori_loop(0, nz, faces, 0)

    for di, dj, copy in s_copies:
        @pl.when(inside(-di, -dj))
        def _():
            copy.wait_recv()

    for zp in range(zp_count):
        for r in WIDE:
            own, left, right = (s[zp, r:r + 8] for s in (s_own, s_left, s_right))
            moved = roll(jnp.where(l16 < 12, left, own), -8)
            b0[zp, r:r + 8] = jnp.where(l16 < 8, moved, jnp.where(l16 < 12, own, right))
            moved = roll(jnp.where(l16 < 4, own, right), 8)
            log = jnp.where(l16 < 8, jnp.where(l16 < 4, left, own), moved)
            ws[zp, r:r + 8] = jnp.exp(-log)
    for zp in range(zp_count):
        for r in WIDE:
            mid = ws[zp, r:r + 8]
            txs[zp, r:r + 8] = 2.0 / (mid + ws[zp, r + 1:r + 9])
            tys[zp, r:r + 8] = 2.0 / (mid + roll(mid, -1))
            if zp < zp_count - 1:
                tzs[zp, r:r + 8] = 2.0 / (mid + ws[zp + 1, r:r + 8])
            else:
                tzs[zp, r:r + 8] = jnp.where(lane < 112, 2.0 / (mid + roll(ws[0, r:r + 8], -16)), 0.0)
    keep_cols = jnp.logical_and(jnp.logical_or(l16 >= 4, j > 0), jnp.logical_or(l16 < 12, j < gy - 1))
    keep_top = jnp.logical_or(sub >= 4, i > 0)
    keep_bottom = jnp.logical_or(sub < 4, i < gx - 1)
    for k in range(4):
        field = strips[k]
        if k < 3:
            for zp in range(zp_count):
                for r in WIDE:
                    mid = field[zp, r:r + 8]
                    above = field[zp + 1, r:r + 8] if zp < zp_count - 1 else roll(field[0, r:r + 8], -16)
                    fzs[zp, r:r + 8] = tzs[zp, r:r + 8] * (mid - above)
        for zp in range(zp_count):
            for r in WIDE:
                mid = field[zp, r:r + 8]
                fy = tys[zp, r:r + 8] * (mid - roll(mid, -1))
                q[k, zp, r:r + 8] = jnp.where(l16 == 8, roll(fy, 5), roll(fy, -4))
                if k == 3:
                    continue
                below = fzs[zp - 1, r:r + 8] if zp else roll(fzs[zp_count - 1, r:r + 8], 16)
                total = txs[zp, r:r + 8] * (mid - field[zp, r + 1:r + 9])
                total = total + txs[zp, r - 1:r + 7] * (mid - field[zp, r - 1:r + 7])
                total = total + (fy - roll(fy, 1)) + (fzs[zp, r:r + 8] - below)
                keep = keep_cols
                if r == 4:
                    keep = jnp.logical_and(keep, keep_top)
                if r == 36:
                    keep = jnp.logical_and(keep, keep_bottom)
                strips[k + 1][zp, r:r + 8] = jnp.where(keep, total, 0.0)

    for step, group in x_copies:
        @pl.when(inside(-step, 0))
        def _():
            for copy in group:
                copy.wait_recv()

    def invert_rim(step, carry):
        for u in range(BLOCK):
            z = BLOCK * step + u
            for h in range(2):
                both = jnp.exp(-jnp.where(sub < 4, lp[h, z, 4:12], lp[h, z, 36:44]))
                w[h, z, 4:8] = both[0:4]
                w[h, z, 40:44] = both[4:8]
        return carry

    lax.fori_loop(0, nz // BLOCK, invert_rim, 0)

    def faces_rim(step, carry):
        layers = []
        for u in range(BLOCK):
            z = BLOCK * step + u
            mids = [jnp.where(sub < 4, w[h, z, 4:12], w[h, z, 35:43]) for h in range(2)]
            edge = [jnp.where(sub < 4, v0[h, z, 4:12], v0[h, z, 36:44]) for h in range(2)]
            layers.append((z, mids, shifted(mids), shifted(edge)))
        for z, mids, (right, left), (more, less) in layers:
            above = jnp.minimum(z + 1, nz - 1)
            top = jnp.where(z < nz - 1, 2.0, 0.0)
            for h, mid in enumerate(mids):
                across = jnp.where(sub < 4, w[h, z, 5:13], w[h, z, 36:44])
                higher = jnp.where(sub < 4, w[h, above, 4:12], w[h, above, 35:43])
                for ref, value in (
                    (tx, 2.0 / (mid + across)),
                    (ty, 2.0 / (mid + right[h])),
                    (tym, 2.0 / (mid + left[h])),
                    (tz, top / (mid + higher)),
                ):
                    ref[h, z, 4:8] = value[0:4]
                    ref[h, z, 39:43] = value[4:8]
                for ref, value in ((yp, more[h]), (ym, less[h])):
                    ref[h, z, 4:8] = value[0:4]
                    ref[h, z, 40:44] = value[4:8]
        return carry

    lax.fori_loop(0, nz // BLOCK, faces_rim, 0)

    for di, dj, copy in s_copies:
        @pl.when(inside(di, dj))
        def _():
            copy.wait_send()
    for step, group in x_copies:
        @pl.when(inside(step, 0))
        def _():
            for copy in group:
                copy.wait_send()


def powers(nz, gx, gy, v0, tx, ty, tz, tym, yp0, ym0, q, v1, v2, v3, v4, coef,
           yp1, ym1, yp2, ym2, sides, send_row, red_a, red_b, a_send, a_recv, c_send, c_recv):
    i = lax.axis_index("gx")
    j = lax.axis_index("gy")
    zp_count = nz // 8
    fields = (v0, v1, v2, v3, v4)
    lane, sub = iota(1), iota(0)
    keep_top = jnp.logical_or(sub >= 4, i > 0)
    keep_bottom = jnp.logical_or(sub < 4, i < gx - 1)

    barrier = pltpu.get_barrier_semaphore()
    for d in range(1, gx):
        pl.semaphore_signal(barrier, inc=1, device_id=(lax.rem(i + d, gx), j), device_id_type=MESH)
    for d in range(1, gy):
        pl.semaphore_signal(barrier, inc=1, device_id=(i, lax.rem(j + d, gy)), device_id_type=MESH)
    for n, red in ((gx, red_a), (gy, red_b)):
        for r in range(n, red.shape[0]):
            red[r:r + 1, :] = jnp.zeros((1, 128), F32)


    steps = nz // BLOCK

    def turned(k, z, r):
        turn = lax.rem(248 - 16 * (z // zp_count), 128)
        return roll(q[k, lax.rem(z, zp_count), r:r + 8], turn)

    moments = []
    for k in range(4):
        src, dst = fields[k], fields[k + 1]
        tiles = WIDE if k < 3 else OWN
        for u in range(BLOCK):
            for n, r in enumerate(tiles):
                sides[0, u, n] = turned(k, u, r)

        def spread(z, dst=dst):
            return [shifted([dst[h, z, r:r + 8] for h in range(2)]) for r in WIDE]

        def settle(z, moved, k=k):
            yp, ym = (yp2, ym2) if k == 1 else (yp1, ym1)
            for r, (right, left) in zip(WIDE, moved):
                for h in range(2):
                    yp[h, z, r:r + 8] = right[h]
                    ym[h, z, r:r + 8] = left[h]

        def block(step, carry, k=k, src=src, dst=dst, tiles=tiles, spread=spread, settle=settle):
            sums, below = list(carry[0]), list(carry[1])
            after, before = ((yp0, ym0), (yp1, ym1), (yp2, ym2), (yp1, ym1))[k]
            now = lax.rem(step, 2)
            moved = {}
            for u in range(BLOCK):
                z = BLOCK * step + u
                last = jnp.maximum(z - BLOCK, u)
                later = jnp.minimum(z + BLOCK, nz - BLOCK + u)
                if k < 3:
                    moved = spread(last)
                fresh = [turned(k, later, r) for r in tiles]
                above = jnp.minimum(z + 1, nz - 1)
                for n, r in enumerate(tiles):
                    rows, up, down = slice(r, r + 8), slice(r + 1, r + 9), slice(r - 1, r + 7)
                    side = sides[now, u, n]
                    for h in range(2):
                        v = src[h, z, rows]
                        ahead = ty[h, z, rows] * (v - after[h, z, rows])
                        back = tym[h, z, rows] * (v - before[h, z, rows])
                        if h == 0:
                            back = jnp.where(lane == 0, -side, back)
                        else:
                            ahead = jnp.where(lane == 127, side, ahead)
                        fz = tz[h, z, rows] * (v - src[h, above, rows])
                        total = tx[h, z, rows] * (v - src[h, z, up])
                        total = total + tx[h, z, down] * (v - src[h, z, down])
                        total = total + (ahead + back) + (fz - below[2 * n + h])
                        below[2 * n + h] = fz
                        mine, new = v, total
                        if r == 4:
                            total = jnp.where(keep_top, total, 0.0)
                            mine = jnp.where(sub >= 4, mine, 0.0)
                            new = jnp.where(sub >= 4, total, 0.0)
                        if r == 36:
                            total = jnp.where(keep_bottom, total, 0.0)
                            mine = jnp.where(sub < 4, mine, 0.0)
                            new = jnp.where(sub < 4, total, 0.0)
                        dst[h, z, rows] = total
                        if k == 0:
                            sums[2] = sums[2] + mine * mine
                        sums[0] = sums[0] + mine * new
                        if k < 3:
                            sums[1] = sums[1] + new * new
                for n in range(len(tiles)):
                    sides[1 - now, u, n] = fresh[n]
                if k < 3:
                    settle(last, moved)
            return tuple(sums), tuple(below)

        zero = jnp.zeros((8, 128), F32)
        count = 3 if k == 0 else 2 if k < 3 else 1
        sums, _ = lax.fori_loop(0, steps, block, ((zero,) * count, (zero,) * (2 * len(tiles))))
        if k < 3:
            for u in range(BLOCK):
                settle(nz - BLOCK + u, spread(nz - BLOCK + u))
        if k == 0:
            moments.append(sums[2])
        moments.extend(sums[:2])

    row = jnp.zeros((8, 128), F32)
    for n, part in enumerate(moments):
        row = jnp.where(lane == n, jnp.sum(part, axis=1, keepdims=True), row)
    row = jnp.sum(row, axis=0, keepdims=True)

    def exchange(value, slot, red, count, send, recv, where):
        send_row[slot:slot + 1, :] = value
        red[0:1, :] = value
        copies = []
        for d in range(1, count):
            copies.append(pltpu.make_async_remote_copy(
                src_ref=send_row.at[pl.ds(slot, 1), :],
                dst_ref=red.at[pl.ds(count - d, 1), :],
                send_sem=send.at[d],
                recv_sem=recv.at[count - d],
                device_id=where(d),
                device_id_type=MESH,
            ))
        for copy in copies:
            copy.start()
        for copy in copies:
            copy.wait_recv()
        return copies

    pl.semaphore_wait(barrier, gx - 1 + gy - 1)
    sent = exchange(row, 0, red_a, gx, a_send, a_recv, lambda d: (lax.rem(i + d, gx), j))
    part = red_a[...]
    hi, lo = tree(part, jnp.zeros_like(part))
    row = jnp.where(lane < 8, hi, pltpu.roll(lo, 8, 1))[0:1]
    sent += exchange(row, 8, red_b, gy, c_send, c_recv, lambda d: (i, lax.rem(j + d, gy)))
    parts = []
    for r in range(0, red_b.shape[0], 8):
        part = red_b[r:r + 8]
        parts.append((part, pltpu.roll(part, 120, 1)))
    total = parts[0]
    for part in parts[1:]:
        total = pair_add(total, part)
    hi, lo = tree(*total)
    splat = [
        (jnp.broadcast_to(hi[:, n:n + 1], (8, 128)), jnp.broadcast_to(lo[:, n:n + 1], (8, 128)))
        for n in range(8)
    ]
    for n, value in enumerate(coefficients(splat)):
        coef[n] = value

    for copy in sent:
        copy.wait_send()


def finish(nz, v0, v1, v2, v3, v4, tx, ty, q, coef, p_out, r_out, e_out, n_out,
           p_buf, r_buf, e_buf, n_buf, wide, side, sems):
    zp_count = nz // 8
    chunk = nz // PARTS
    lane = iota(1)
    c = [coef[n] for n in range(4)]

    def combine(parts):
        return (c[0] * parts[0] + c[1] * parts[1]) + (c[2] * parts[2] + c[3] * parts[3])

    for zp in range(zp_count):
        for r in OWN:
            side[zp, r:r + 8] = combine([q[k, zp, r:r + 8] for k in range(4)])

    def block(step, carry):
        moved = {}

        def first(u):
            z = BLOCK * step + u
            turn = lax.rem(248 - 16 * (z // zp_count), 128)
            for r in OWN:
                press = []
                for h in range(2):
                    v = [f[h, z, r:r + 8] for f in (v0, v1, v2, v3)]
                    press.append(combine(v))
                    wide[u, h, r:r + 8] = press[h]
                    cols = slice(128 * h, 128 * h + 128)
                    p_buf[z, r - 8:r, cols] = press[h]
                    r_buf[z, r - 8:r, cols] = v[0] - combine(v[1:] + [v4[h, z, r:r + 8]])
                moved[u, r] = [roll(p, -1) for p in press]
                moved[u, r].append(roll(side[lax.rem(z, zp_count), r:r + 8], turn))
            for h in range(2):
                wide[u, h, 40:48] = combine([f[h, z, 40:48] for f in (v0, v1, v2, v3)])

        def second(u):
            z = BLOCK * step + u
            for r in OWN:
                one, two, rim = moved[u, r]
                for h, across in ((0, jnp.where(lane == 127, two, one)), (1, two)):
                    cols = slice(128 * h, 128 * h + 128)
                    press = wide[u, h, r:r + 8]
                    e_buf[z, r - 8:r, cols] = tx[h, z, r:r + 8] * (press - wide[u, h, r + 1:r + 9])
                    north = ty[h, z, r:r + 8] * (press - across)
                    if h == 1:
                        north = jnp.where(lane == 127, rim, north)
                    n_buf[z, r - 8:r, cols] = north

        for u in range(BLOCK):
            first(u)
            if u:
                second(u - 1)
        second(BLOCK - 1)
        return carry

    copies = []
    for part in range(PARTS):
        lax.fori_loop(part * chunk // BLOCK, (part + 1) * chunk // BLOCK, block, 0)
        for n, (buf, out) in enumerate(((p_buf, p_out), (r_buf, r_out), (e_buf, e_out), (n_buf, n_out))):
            copy = pltpu.make_async_copy(
                buf.at[pl.ds(part * chunk, chunk)],
                out.at[0, pl.ds(part * chunk, chunk)],
                sems.at[4 * part + n],
            )
            copy.start()
            copies.append(copy)
    for copy in copies:
        copy.wait()


def solution(mesh):
    gx, gy = mesh.shape["gx"], mesh.shape["gy"]

    def on_device(log_perm, source):
        nz = log_perm.shape[1]
        zp = nz // 8
        field = (2, nz, ROWS, 128)
        strip = (zp, ROWS, 128)
        vmem = pl.BlockSpec(memory_space=pltpu.VMEM)
        hbm = pl.BlockSpec(memory_space=pltpu.HBM)
        made = pl.pallas_call(
            functools.partial(gather, nz, gx, gy),
            out_shape=[pltpu.VMEM(field, F32)] * 7 + [pltpu.VMEM((4,) + strip, F32)],
            in_specs=[hbm] * 2,
            out_specs=[vmem] * 8,
            scratch_shapes=[pltpu.VMEM(field, F32)] * 2
            + [pltpu.VMEM(strip, F32)] * 12
            + [pltpu.SemaphoreType.DMA((4,))]
            + [pltpu.SemaphoreType.DMA((8,))] * 4,
            compiler_params=pltpu.CompilerParams(
                collective_id=0, has_side_effects=True, vmem_limit_bytes=16 << 20
            ),
            name="gather",
        )(*(pltpu.with_memory_space_constraint(x, pltpu.HBM) for x in (log_perm, source)))
        v0, tx, ty, tz, tym, yp, ym, q = made
        v1, v2, v3, v4, coef = pl.pallas_call(
            functools.partial(powers, nz, gx, gy),
            out_shape=[pltpu.VMEM(field, F32)] * 4 + [pltpu.VMEM((4, 8, 128), F32)],
            in_specs=[vmem] * 8,
            out_specs=[vmem] * 5,
            scratch_shapes=[pltpu.VMEM(field, F32)] * 4
            + [
                pltpu.VMEM((2, BLOCK, 5, 8, 128), F32),
                pltpu.VMEM((16, 128), F32),
                pltpu.VMEM((8, 128), F32),
                pltpu.VMEM((max(8, gy), 128), F32),
            ]
            + [pltpu.SemaphoreType.DMA((gx,))] * 2
            + [pltpu.SemaphoreType.DMA((gy,))] * 2,
            compiler_params=pltpu.CompilerParams(
                collective_id=1, has_side_effects=True, vmem_limit_bytes=14 << 20
            ),
            name="powers",
        )(*made)
        shape = jax.ShapeDtypeStruct(log_perm.shape, F32)
        return pl.pallas_call(
            functools.partial(finish, nz),
            out_shape=[shape] * 4,
            in_specs=[vmem] * 9,
            out_specs=[hbm] * 4,
            scratch_shapes=[pltpu.VMEM((nz, 32, 256), F32)] * 4
            + [pltpu.VMEM((BLOCK, 2, ROWS, 128), F32), pltpu.VMEM(strip, F32), pltpu.SemaphoreType.DMA((4 * PARTS,))],
            compiler_params=pltpu.CompilerParams(vmem_limit_bytes=12 << 20),
            name="finish",
        )(v0, v1, v2, v3, v4, tx, ty, q, coef)

    spec = P(None, None, "gx", "gy")
    return jax.shard_map(
        on_device, mesh=mesh, in_specs=(spec, spec), out_specs=(spec,) * 4, check_vma=False
    )
```

```python
import functools

import jax
import jax.numpy as jnp
from jax import lax
from jax.experimental import pallas as pl
from jax.experimental.pallas import tpu as pltpu
from jax.sharding import PartitionSpec as P

MESH = pl.DeviceIdType.MESH
F32 = jnp.float32
TOP = 8
ROWS = 48
WIDE = (4, 12, 20, 28, 36)
OWN = (8, 16, 24, 32)
PARTS = 4
BLOCK = 4
DIRS = ((0, 1), (0, -1), (1, 0), (-1, 0), (1, 1), (1, -1), (-1, 1), (-1, -1))


def iota(dim):
    return lax.broadcasted_iota(jnp.int32, (8, 128), dim)


def roll(value, amount):
    return pltpu.roll(value, amount % 128 if isinstance(amount, int) else amount, 1)


def two_sum(a, b):
    s = a + b
    t = s - a
    return s, (a - (s - t)) + (b - t)


def quick(a, b):
    s = a + b
    return s, b - (s - a)


def pair_add(x, y):
    s, e = two_sum(x[0], y[0])
    return quick(s, e + (x[1] + y[1]))


def halves(a):
    t = a * 4097.0
    hi = t - (t - a)
    return hi, a - hi


def pair_mul(x, y):
    p = x[0] * y[0]
    xh, xl = halves(x[0])
    yh, yl = halves(y[0])
    e = ((xh * yh - p) + xh * yl + xl * yh) + xl * yl
    return quick(p, e + (x[0] * y[1] + x[1] * y[0]))


def neg(x):
    return (-x[0], -x[1])


def pair_div(x, y):
    q = x[0] / y[0]
    zero = jnp.zeros_like(q)
    rest = pair_add(x, neg(pair_mul(y, (q, zero))))
    return quick(q, rest[0] / y[0])


def coefficients(moments):
    resid, direc = dict(enumerate(moments)), dict(enumerate(moments))
    steps, ratios = [], []
    for k in range(4):
        step = pair_div(resid[k], direc[k + 1])
        steps.append(step)
        if k == 3:
            break
        fresh = {}
        for l in range(k + 1, 7 - k):
            fresh[l] = pair_add(resid[l], neg(pair_mul(step, direc[l + 1])))
        ratio = neg(pair_div(pair_mul(step, fresh[k + 1]), resid[k]))
        ratios.append(ratio)
        direc = {l: pair_add(fresh[l], pair_mul(ratio, direc[l])) for l in fresh}
        resid = fresh
    a = [s[0] for s in steps]
    b = [r[0] for r in ratios]
    one = jnp.ones_like(a[0])
    r, p = [one], [one]
    x = [a[0]]
    for k in range(3):
        moved = [None] + [a[k] * c for c in p]
        r = [
            moved[m] * -1.0 if m >= len(r) else (r[m] if moved[m] is None else r[m] - moved[m])
            for m in range(len(moved))
        ]
        p = [r[m] + b[k] * p[m] if m < len(p) else r[m] for m in range(len(r))]
        x = [x[m] + a[k + 1] * p[m] if m < len(x) else a[k + 1] * p[m] for m in range(len(p))]
    return x


def shifted(pair):
    lane = iota(1)
    right = [roll(p, -1) for p in pair]
    left = [roll(p, 1) for p in pair]
    right[0] = jnp.where(lane == 127, right[1], right[0])
    left[1] = jnp.where(lane == 0, left[0], left[1])
    return right, left


def tree(hi, lo):
    for shift in (4, 2, 1):
        hi, lo = pair_add((hi, lo), (pltpu.roll(hi, shift, 0), pltpu.roll(lo, shift, 0)))
    return hi, lo


def gather(nz, gx, gy, lp_ref, src_ref, v0, tx, ty, tz, tym, yp, ym, q,
           lp, w, s_own, s_left, s_right, to_right, to_left, ws, txs, tys, tzs, b0, b1, b2, b3, fzs,
           load_sem, x_send, x_recv, s_send, s_recv):
    i = lax.axis_index("gx")
    j = lax.axis_index("gy")
    zp_count = nz // 8
    strips = (b0, b1, b2, b3)
    lane, sub = iota(1), iota(0)
    l16, l8 = lane % 16, lane % 8

    def inside(di, dj):
        ok = None
        for cond in (
            [] if di == 0 else [i < gx - 1] if di > 0 else [i > 0]
        ) + ([] if dj == 0 else [j < gy - 1] if dj > 0 else [j > 0]):
            ok = cond if ok is None else jnp.logical_and(ok, cond)
        return ok

    loads = []
    for n, (source, target) in enumerate(((src_ref, v0), (lp_ref, lp))):
        for h in range(2):
            copy = pltpu.make_async_copy(
                source.at[0, :, :, pl.ds(128 * h, 128)],
                target.at[h, :, pl.ds(TOP, 32), :],
                load_sem.at[2 * n + h],
            )
            copy.start()
            loads.append(copy)

    barrier = pltpu.get_barrier_semaphore()
    for di, dj in DIRS:
        @pl.when(inside(di, dj))
        def _():
            pl.semaphore_signal(barrier, inc=1, device_id=(i + di, j + dj), device_id_type=MESH)

    zero4 = jnp.zeros((4, 128), F32)

    @pl.when(i == 0)
    def _():
        def fill(z, carry):
            for h in range(2):
                v0[h, z, 4:8] = zero4
                lp[h, z, 4:8] = zero4
            return carry
        lax.fori_loop(0, nz, fill, 0)
        for buf in (s_own, s_left, s_right):
            for zp in range(buf.shape[0]):
                buf[zp, 4:8] = zero4

    @pl.when(i == gx - 1)
    def _():
        def fill(z, carry):
            for h in range(2):
                v0[h, z, 40:44] = zero4
                lp[h, z, 40:44] = zero4
            return carry
        lax.fori_loop(0, nz, fill, 0)
        for buf in (s_own, s_left, s_right):
            for zp in range(buf.shape[0]):
                buf[zp, 40:44] = zero4

    for edge, buf in ((j == 0, s_left), (j == gy - 1, s_right)):
        @pl.when(edge)
        def _():
            for zp in range(zp_count // 2):
                buf[zp, 4:8] = zero4
                buf[zp, 40:44] = zero4
                for r in OWN:
                    buf[zp, r:r + 8] = jnp.zeros((8, 128), F32)

    inner_i = (i > 0).astype(jnp.int32) + (i < gx - 1).astype(jnp.int32)
    inner_j = (j > 0).astype(jnp.int32) + (j < gy - 1).astype(jnp.int32)
    pl.semaphore_wait(barrier, inner_i + inner_j + inner_i * inner_j)

    x_copies = []
    for step, first, land in ((1, 28, 4), (-1, 0, 40)):
        group = []
        for n, (source, target) in enumerate(((lp_ref, lp), (src_ref, v0))):
            for h in range(2):
                slot = (0 if step > 0 else 4) + 2 * n + h
                group.append(pltpu.make_async_remote_copy(
                    src_ref=source.at[0, :, pl.ds(first, 4), pl.ds(128 * h, 128)],
                    dst_ref=target.at[h, :, pl.ds(land, 4), :],
                    send_sem=x_send.at[slot],
                    recv_sem=x_recv.at[slot],
                    device_id=(i + step, j),
                    device_id_type=MESH,
                ))
        x_copies.append((step, group))

        @pl.when(inside(step, 0))
        def _():
            for copy in group:
                copy.start()

    for copy in loads:
        copy.wait()

    def pack(pair, carry):
        for r in OWN:
            planes = []
            for u in range(2):
                packed = jnp.zeros((8, 128), F32)
                for g in range(8):
                    z = g * zp_count + 2 * pair + u
                    fld = jnp.where(lane < 64, v0[0, z, r:r + 8], v0[1, z, r:r + 8])
                    log = jnp.where(lane < 64, lp[0, z, r:r + 8], lp[1, z, r:r + 8])
                    both = jnp.where(l16 < 8, roll(log, 16 * g + 4), roll(fld, 16 * g + 12))
                    packed = jnp.where(lane // 16 == g, both, packed)
                s_own[2 * pair + u, r:r + 8] = packed
                planes.append(packed)
            to_right[pair, r:r + 8] = jnp.where(l8 < 4, planes[0], roll(planes[1], 4))
            to_left[pair, r:r + 8] = jnp.where(l8 < 4, roll(planes[1], -4), planes[0])
        return carry

    lax.fori_loop(0, zp_count // 2, pack, 0)

    s_copies = []
    for n, (di, dj) in enumerate(DIRS):
        base = s_own if dj == 0 else to_right if dj > 0 else to_left
        target = s_own if dj == 0 else s_left if dj > 0 else s_right
        if di == 0:
            first, land, count = 8, 8, 32
        elif di > 0:
            first, land, count = 36, 4, 4
        else:
            first, land, count = 8, 40, 4
        copy = pltpu.make_async_remote_copy(
            src_ref=base.at[:, pl.ds(first, count), :],
            dst_ref=target.at[:, pl.ds(land, count), :],
            send_sem=s_send.at[n],
            recv_sem=s_recv.at[n],
            device_id=(i + di, j + dj),
            device_id_type=MESH,
        )
        s_copies.append((di, dj, copy))

    for di, dj, copy in s_copies[4:] + s_copies[:4]:
        @pl.when(inside(di, dj))
        def _():
            copy.start()

    def invert(step, carry):
        for u in range(BLOCK):
            for h in range(2):
                for r in OWN:
                    z = BLOCK * step + u
                    w[h, z, r:r + 8] = jnp.exp(-lp[h, z, r:r + 8])
        return carry

    lax.fori_loop(0, nz // BLOCK, invert, 0)

    def faces(step, carry):
        for u in range(BLOCK):
            z = BLOCK * step + u
            above = jnp.minimum(z + 1, nz - 1)
            top = jnp.where(z < nz - 1, 2.0, 0.0)
            for r in OWN:
                mids = [w[h, z, r:r + 8] for h in range(2)]
                right, left = shifted(mids)
                more, less = shifted([v0[h, z, r:r + 8] for h in range(2)])
                for h, mid in enumerate(mids):
                    ty[h, z, r:r + 8] = 2.0 / (mid + right[h])
                    tym[h, z, r:r + 8] = 2.0 / (mid + left[h])
                    tx[h, z, r:r + 8] = 2.0 / (mid + w[h, z, r + 1:r + 9])
                    tz[h, z, r:r + 8] = top / (mid + w[h, above, r:r + 8])
                    yp[h, z, r:r + 8] = more[h]
                    ym[h, z, r:r + 8] = less[h]
        return carry

    lax.fori_loop(0, nz // BLOCK, faces, 0)

    for step, group in x_copies:
        @pl.when(inside(-step, 0))
        def _():
            for copy in group[:2]:
                copy.wait_recv()

    def invert_rim(step, carry):
        for u in range(BLOCK):
            z = BLOCK * step + u
            for h in range(2):
                both = jnp.exp(-jnp.where(sub < 4, lp[h, z, 4:12], lp[h, z, 36:44]))
                w[h, z, 4:8] = both[0:4]
                w[h, z, 40:44] = both[4:8]
        return carry

    lax.fori_loop(0, nz // BLOCK, invert_rim, 0)

    def faces_rim(step, carry):
        layers = []
        for u in range(BLOCK):
            z = BLOCK * step + u
            mids = [jnp.where(sub < 4, w[h, z, 4:12], w[h, z, 35:43]) for h in range(2)]
            layers.append((z, mids, shifted(mids)))
        for z, mids, (right, left) in layers:
            above = jnp.minimum(z + 1, nz - 1)
            top = jnp.where(z < nz - 1, 2.0, 0.0)
            for h, mid in enumerate(mids):
                across = jnp.where(sub < 4, w[h, z, 5:13], w[h, z, 36:44])
                higher = jnp.where(sub < 4, w[h, above, 4:12], w[h, above, 35:43])
                for ref, value in (
                    (tx, 2.0 / (mid + across)),
                    (ty, 2.0 / (mid + right[h])),
                    (tym, 2.0 / (mid + left[h])),
                    (tz, top / (mid + higher)),
                ):
                    ref[h, z, 4:8] = value[0:4]
                    ref[h, z, 39:43] = value[4:8]
        return carry

    lax.fori_loop(0, nz // BLOCK, faces_rim, 0)

    for step, group in x_copies:
        @pl.when(inside(-step, 0))
        def _():
            for copy in group[2:]:
                copy.wait_recv()

    def moved_rim(step, carry):
        layers = []
        for u in range(BLOCK):
            z = BLOCK * step + u
            layers.append((z, shifted([jnp.where(sub < 4, v0[h, z, 4:12], v0[h, z, 36:44]) for h in range(2)])))
        for z, (more, less) in layers:
            for h in range(2):
                for ref, value in ((yp, more[h]), (ym, less[h])):
                    ref[h, z, 4:8] = value[0:4]
                    ref[h, z, 40:44] = value[4:8]
        return carry

    lax.fori_loop(0, nz // BLOCK, moved_rim, 0)

    for di, dj, copy in s_copies:
        @pl.when(inside(-di, -dj))
        def _():
            copy.wait_recv()

    for zp in range(zp_count):
        for r in WIDE:
            own, left, right = s_own[zp, r:r + 8], s_left[zp // 2, r:r + 8], s_right[zp // 2, r:r + 8]
            if zp % 2:
                left, right = roll(left, -4), roll(right, 4)
            moved = roll(jnp.where(l16 < 12, left, own), -8)
            b0[zp, r:r + 8] = jnp.where(l16 < 8, moved, jnp.where(l16 < 12, own, right))
            moved = roll(jnp.where(l16 < 4, own, right), 8)
            log = jnp.where(l16 < 8, jnp.where(l16 < 4, left, own), moved)
            ws[zp, r:r + 8] = jnp.exp(-log)
    for zp in range(zp_count):
        for r in WIDE:
            mid = ws[zp, r:r + 8]
            txs[zp, r:r + 8] = 2.0 / (mid + ws[zp, r + 1:r + 9])
            tys[zp, r:r + 8] = 2.0 / (mid + roll(mid, -1))
            if zp < zp_count - 1:
                tzs[zp, r:r + 8] = 2.0 / (mid + ws[zp + 1, r:r + 8])
            else:
                tzs[zp, r:r + 8] = jnp.where(lane < 112, 2.0 / (mid + roll(ws[0, r:r + 8], -16)), 0.0)
    keep_cols = jnp.logical_and(jnp.logical_or(l16 >= 4, j > 0), jnp.logical_or(l16 < 12, j < gy - 1))
    keep_top = jnp.logical_or(sub >= 4, i > 0)
    keep_bottom = jnp.logical_or(sub < 4, i < gx - 1)
    for k in range(4):
        field = strips[k]
        if k < 3:
            for zp in range(zp_count):
                for r in WIDE:
                    mid = field[zp, r:r + 8]
                    above = field[zp + 1, r:r + 8] if zp < zp_count - 1 else roll(field[0, r:r + 8], -16)
                    fzs[zp, r:r + 8] = tzs[zp, r:r + 8] * (mid - above)
        for zp in range(zp_count):
            for r in WIDE:
                mid = field[zp, r:r + 8]
                fy = tys[zp, r:r + 8] * (mid - roll(mid, -1))
                q[k, zp, r:r + 8] = jnp.where(l16 == 8, roll(fy, 5), roll(fy, -4))
                if k == 3:
                    continue
                below = fzs[zp - 1, r:r + 8] if zp else roll(fzs[zp_count - 1, r:r + 8], 16)
                total = txs[zp, r:r + 8] * (mid - field[zp, r + 1:r + 9])
                total = total + txs[zp, r - 1:r + 7] * (mid - field[zp, r - 1:r + 7])
                total = total + (fy - roll(fy, 1)) + (fzs[zp, r:r + 8] - below)
                keep = keep_cols
                if r == 4:
                    keep = jnp.logical_and(keep, keep_top)
                if r == 36:
                    keep = jnp.logical_and(keep, keep_bottom)
                strips[k + 1][zp, r:r + 8] = jnp.where(keep, total, 0.0)

    for di, dj, copy in s_copies:
        @pl.when(inside(di, dj))
        def _():
            copy.wait_send()
    for step, group in x_copies:
        @pl.when(inside(step, 0))
        def _():
            for copy in group:
                copy.wait_send()


def powers(nz, gx, gy, v0, tx, ty, tz, tym, yp0, ym0, q, v1, v2, v3, v4, coef,
           yp1, ym1, yp2, ym2, sides, send_row, red_a, red_b, a_send, a_recv, c_send, c_recv):
    i = lax.axis_index("gx")
    j = lax.axis_index("gy")
    zp_count = nz // 8
    fields = (v0, v1, v2, v3, v4)
    lane, sub = iota(1), iota(0)
    keep_top = jnp.logical_or(sub >= 4, i > 0)
    keep_bottom = jnp.logical_or(sub < 4, i < gx - 1)

    barrier = pltpu.get_barrier_semaphore()
    for d in range(1, gx):
        pl.semaphore_signal(barrier, inc=1, device_id=(lax.rem(i + d, gx), j), device_id_type=MESH)
    for d in range(1, gy):
        pl.semaphore_signal(barrier, inc=1, device_id=(i, lax.rem(j + d, gy)), device_id_type=MESH)
    for n, red in ((gx, red_a), (gy, red_b)):
        for r in range(n, red.shape[0]):
            red[r:r + 1, :] = jnp.zeros((1, 128), F32)


    steps = nz // BLOCK

    def turned(k, z, r):
        turn = lax.rem(248 - 16 * (z // zp_count), 128)
        return roll(q[k, lax.rem(z, zp_count), r:r + 8], turn)

    row = jnp.zeros((8, 128), F32)
    found = 0
    for k in range(4):
        src, dst = fields[k], fields[k + 1]
        tiles = WIDE if k < 3 else OWN
        for u in range(BLOCK):
            for n, r in enumerate(tiles):
                sides[0, u, n] = turned(k, u, r)

        def spread(z, dst=dst):
            return [shifted([dst[h, z, r:r + 8] for h in range(2)]) for r in WIDE]

        def settle(z, moved, k=k):
            yp, ym = (yp2, ym2) if k == 1 else (yp1, ym1)
            for r, (right, left) in zip(WIDE, moved):
                for h in range(2):
                    yp[h, z, r:r + 8] = right[h]
                    ym[h, z, r:r + 8] = left[h]

        def block(step, carry, k=k, src=src, dst=dst, tiles=tiles, spread=spread, settle=settle):
            sums, below = list(carry[0]), list(carry[1])
            after, before = ((yp0, ym0), (yp1, ym1), (yp2, ym2), (yp1, ym1))[k]
            now = lax.rem(step, 2)
            moved = {}
            for u in range(BLOCK):
                z = BLOCK * step + u
                last = jnp.maximum(z - BLOCK, u)
                later = jnp.minimum(z + BLOCK, nz - BLOCK + u)
                if k < 3:
                    moved = spread(last)
                fresh = [turned(k, later, r) for r in tiles]
                above = jnp.minimum(z + 1, nz - 1)
                for n, r in enumerate(tiles):
                    rows, up, down = slice(r, r + 8), slice(r + 1, r + 9), slice(r - 1, r + 7)
                    side = sides[now, u, n]
                    for h in range(2):
                        v = src[h, z, rows]
                        ahead = ty[h, z, rows] * (v - after[h, z, rows])
                        back = tym[h, z, rows] * (v - before[h, z, rows])
                        if h == 0:
                            back = jnp.where(lane == 0, -side, back)
                        else:
                            ahead = jnp.where(lane == 127, side, ahead)
                        fz = tz[h, z, rows] * (v - src[h, above, rows])
                        total = tx[h, z, rows] * (v - src[h, z, up])
                        total = total + tx[h, z, down] * (v - src[h, z, down])
                        total = total + (ahead + back) + (fz - below[2 * n + h])
                        below[2 * n + h] = fz
                        mine, new = v, total
                        if r == 4:
                            total = jnp.where(keep_top, total, 0.0)
                            mine = jnp.where(sub >= 4, mine, 0.0)
                            new = jnp.where(sub >= 4, total, 0.0)
                        if r == 36:
                            total = jnp.where(keep_bottom, total, 0.0)
                            mine = jnp.where(sub < 4, mine, 0.0)
                            new = jnp.where(sub < 4, total, 0.0)
                        dst[h, z, rows] = total
                        if k == 0:
                            sums[2] = sums[2] + mine * mine
                        sums[0] = sums[0] + mine * new
                        if k < 3:
                            sums[1] = sums[1] + new * new
                for n in range(len(tiles)):
                    sides[1 - now, u, n] = fresh[n]
                if k < 3:
                    settle(last, moved)
            return tuple(sums), tuple(below)

        zero = jnp.zeros((8, 128), F32)
        count = 3 if k == 0 else 2 if k < 3 else 1
        sums, _ = lax.fori_loop(0, steps, block, ((zero,) * count, (zero,) * (2 * len(tiles))))
        if k < 3:
            for u in range(BLOCK):
                settle(nz - BLOCK + u, spread(nz - BLOCK + u))
        for part in ([sums[2]] if k == 0 else []) + list(sums[:2]):
            row = jnp.where(lane == found, jnp.sum(part, axis=1, keepdims=True), row)
            found += 1

    row = jnp.sum(row, axis=0, keepdims=True)

    def exchange(value, slot, red, count, send, recv, where):
        send_row[slot:slot + 1, :] = value
        red[0:1, :] = value
        copies = []
        far = (lambda d: -min(d, count - d)) if count == gx else (
            lambda d: -min(d % 4, 4 - d % 4) - min(d // 4, 4 - d // 4))
        for d in sorted(range(1, count), key=far):
            copies.append(pltpu.make_async_remote_copy(
                src_ref=send_row.at[pl.ds(slot, 1), :],
                dst_ref=red.at[pl.ds(count - d, 1), :],
                send_sem=send.at[d],
                recv_sem=recv.at[count - d],
                device_id=where(d),
                device_id_type=MESH,
            ))
        for copy in copies:
            copy.start()
        for copy in copies:
            copy.wait_recv()
        return copies

    pl.semaphore_wait(barrier, gx - 1 + gy - 1)
    sent = exchange(row, 0, red_a, gx, a_send, a_recv, lambda d: (lax.rem(i + d, gx), j))
    part = red_a[...]
    hi, lo = tree(part, jnp.zeros_like(part))
    row = jnp.where(lane < 8, hi, pltpu.roll(lo, 8, 1))[0:1]
    sent += exchange(row, 8, red_b, gy, c_send, c_recv, lambda d: (i, lax.rem(j + d, gy)))
    parts = []
    for r in range(0, red_b.shape[0], 8):
        part = red_b[r:r + 8]
        parts.append((part, pltpu.roll(part, 120, 1)))
    total = parts[0]
    for part in parts[1:]:
        total = pair_add(total, part)
    hi, lo = tree(*total)
    splat = [
        (jnp.broadcast_to(hi[:, n:n + 1], (8, 128)), jnp.broadcast_to(lo[:, n:n + 1], (8, 128)))
        for n in range(8)
    ]
    for n, value in enumerate(coefficients(splat)):
        coef[n] = value

    for copy in sent:
        copy.wait_send()


def finish(nz, v0, v1, v2, v3, v4, tx, ty, q, coef, p_out, r_out, e_out, n_out,
           p_buf, r_buf, e_buf, n_buf, wide, side, sems):
    zp_count = nz // 8
    chunk = nz // PARTS
    lane = iota(1)
    c = [coef[n] for n in range(4)]

    def combine(parts):
        return (c[0] * parts[0] + c[1] * parts[1]) + (c[2] * parts[2] + c[3] * parts[3])

    for zp in range(zp_count):
        for r in OWN:
            side[zp, r:r + 8] = combine([q[k, zp, r:r + 8] for k in range(4)])

    def block(step, carry):
        moved = {}

        def first(u):
            z = BLOCK * step + u
            turn = lax.rem(248 - 16 * (z // zp_count), 128)
            for r in OWN:
                press = []
                for h in range(2):
                    v = [f[h, z, r:r + 8] for f in (v0, v1, v2, v3)]
                    press.append(combine(v))
                    wide[u, h, r:r + 8] = press[h]
                    cols = slice(128 * h, 128 * h + 128)
                    p_buf[z, r - 8:r, cols] = press[h]
                    r_buf[z, r - 8:r, cols] = v[0] - combine(v[1:] + [v4[h, z, r:r + 8]])
                moved[u, r] = [roll(p, -1) for p in press]
                moved[u, r].append(roll(side[lax.rem(z, zp_count), r:r + 8], turn))
            for h in range(2):
                wide[u, h, 40:48] = combine([f[h, z, 40:48] for f in (v0, v1, v2, v3)])

        def second(u):
            z = BLOCK * step + u
            for r in OWN:
                one, two, rim = moved[u, r]
                for h, across in ((0, jnp.where(lane == 127, two, one)), (1, two)):
                    cols = slice(128 * h, 128 * h + 128)
                    press = wide[u, h, r:r + 8]
                    e_buf[z, r - 8:r, cols] = tx[h, z, r:r + 8] * (press - wide[u, h, r + 1:r + 9])
                    north = ty[h, z, r:r + 8] * (press - across)
                    if h == 1:
                        north = jnp.where(lane == 127, rim, north)
                    n_buf[z, r - 8:r, cols] = north

        for u in range(BLOCK):
            first(u)
            if u:
                second(u - 1)
        second(BLOCK - 1)
        return carry

    copies = []
    for part in range(PARTS):
        lax.fori_loop(part * chunk // BLOCK, (part + 1) * chunk // BLOCK, block, 0)
        for n, (buf, out) in enumerate(((p_buf, p_out), (r_buf, r_out), (e_buf, e_out), (n_buf, n_out))):
            copy = pltpu.make_async_copy(
                buf.at[pl.ds(part * chunk, chunk)],
                out.at[0, pl.ds(part * chunk, chunk)],
                sems.at[4 * part + n],
            )
            copy.start()
            copies.append(copy)
    for copy in copies:
        copy.wait()


def solution(mesh):
    gx, gy = mesh.shape["gx"], mesh.shape["gy"]

    def on_device(log_perm, source):
        nz = log_perm.shape[1]
        zp = nz // 8
        field = (2, nz, ROWS, 128)
        strip = (zp, ROWS, 128)
        vmem = pl.BlockSpec(memory_space=pltpu.VMEM)
        hbm = pl.BlockSpec(memory_space=pltpu.HBM)
        made = pl.pallas_call(
            functools.partial(gather, nz, gx, gy),
            out_shape=[pltpu.VMEM(field, F32)] * 7 + [pltpu.VMEM((4,) + strip, F32)],
            in_specs=[hbm] * 2,
            out_specs=[vmem] * 8,
            scratch_shapes=[pltpu.VMEM(field, F32)] * 2
            + [pltpu.VMEM(strip, F32)]
            + [pltpu.VMEM((zp // 2, ROWS, 128), F32)] * 4
            + [pltpu.VMEM(strip, F32)] * 9
            + [pltpu.SemaphoreType.DMA((4,))]
            + [pltpu.SemaphoreType.DMA((8,))] * 4,
            compiler_params=pltpu.CompilerParams(
                collective_id=0, has_side_effects=True, vmem_limit_bytes=16 << 20
            ),
            name="gather",
        )(*(pltpu.with_memory_space_constraint(x, pltpu.HBM) for x in (log_perm, source)))
        v0, tx, ty, tz, tym, yp, ym, q = made
        v1, v2, v3, v4, coef = pl.pallas_call(
            functools.partial(powers, nz, gx, gy),
            out_shape=[pltpu.VMEM(field, F32)] * 4 + [pltpu.VMEM((4, 8, 128), F32)],
            in_specs=[vmem] * 8,
            out_specs=[vmem] * 5,
            scratch_shapes=[pltpu.VMEM(field, F32)] * 4
            + [
                pltpu.VMEM((2, BLOCK, 5, 8, 128), F32),
                pltpu.VMEM((16, 128), F32),
                pltpu.VMEM((8, 128), F32),
                pltpu.VMEM((max(8, gy), 128), F32),
            ]
            + [pltpu.SemaphoreType.DMA((gx,))] * 2
            + [pltpu.SemaphoreType.DMA((gy,))] * 2,
            compiler_params=pltpu.CompilerParams(
                collective_id=1, has_side_effects=True, vmem_limit_bytes=14 << 20
            ),
            name="powers",
        )(*made)
        shape = jax.ShapeDtypeStruct(log_perm.shape, F32)
        return pl.pallas_call(
            functools.partial(finish, nz),
            out_shape=[shape] * 4,
            in_specs=[vmem] * 9,
            out_specs=[hbm] * 4,
            scratch_shapes=[pltpu.VMEM((nz, 32, 256), F32)] * 4
            + [pltpu.VMEM((BLOCK, 2, ROWS, 128), F32), pltpu.VMEM(strip, F32), pltpu.SemaphoreType.DMA((4 * PARTS,))],
            compiler_params=pltpu.CompilerParams(vmem_limit_bytes=12 << 20),
            name="finish",
        )(v0, v1, v2, v3, v4, tx, ty, q, coef)

    spec = P(None, None, "gx", "gy")
    return jax.shard_map(
        on_device, mesh=mesh, in_specs=(spec, spec), out_specs=(spec,) * 4, check_vma=False
    )
```

```python
import functools

import jax
import jax.numpy as jnp
from jax import lax
from jax.experimental import pallas as pl
from jax.experimental.pallas import tpu as pltpu
from jax.sharding import PartitionSpec as P

MESH = pl.DeviceIdType.MESH
F32 = jnp.float32
TOP = 8
ROWS = 48
WIDE = (4, 12, 20, 28, 36)
OWN = (8, 16, 24, 32)
PARTS = 4
BLOCK = 4
DIRS = ((0, 1), (0, -1), (1, 0), (-1, 0), (1, 1), (1, -1), (-1, 1), (-1, -1))


def iota(dim):
    return lax.broadcasted_iota(jnp.int32, (8, 128), dim)


def roll(value, amount):
    return pltpu.roll(value, amount % 128 if isinstance(amount, int) else amount, 1)


def two_sum(a, b):
    s = a + b
    t = s - a
    return s, (a - (s - t)) + (b - t)


def quick(a, b):
    s = a + b
    return s, b - (s - a)


def pair_add(x, y):
    s, e = two_sum(x[0], y[0])
    return quick(s, e + (x[1] + y[1]))


def halves(a):
    t = a * 4097.0
    hi = t - (t - a)
    return hi, a - hi


def pair_mul(x, y):
    p = x[0] * y[0]
    xh, xl = halves(x[0])
    yh, yl = halves(y[0])
    e = ((xh * yh - p) + xh * yl + xl * yh) + xl * yl
    return quick(p, e + (x[0] * y[1] + x[1] * y[0]))


def neg(x):
    return (-x[0], -x[1])


def pair_div(x, y):
    q = x[0] / y[0]
    p = q * y[0]
    qh, ql = halves(q)
    yh, yl = halves(y[0])
    e = ((qh * yh - p) + qh * yl + ql * yh) + ql * yl
    rest = ((x[0] - p) - (e + q * y[1])) + x[1]
    return quick(q, rest / y[0])


def coefficients(moments):
    resid, direc = dict(enumerate(moments)), dict(enumerate(moments))
    steps, ratios = [], []
    for k in range(4):
        step = pair_div(resid[k], direc[k + 1])
        steps.append(step)
        if k == 3:
            break
        fresh = {}
        for l in range(k + 1, 7 - k):
            fresh[l] = pair_add(resid[l], neg(pair_mul(step, direc[l + 1])))
        ratio = neg(pair_div(pair_mul(step, fresh[k + 1]), resid[k]))
        ratios.append(ratio)
        direc = {l: pair_add(fresh[l], pair_mul(ratio, direc[l])) for l in fresh}
        resid = fresh
    a = [s[0] for s in steps]
    b = [r[0] for r in ratios]
    one = jnp.ones_like(a[0])
    r, p = [one], [one]
    x = [a[0]]
    for k in range(3):
        moved = [None] + [a[k] * c for c in p]
        r = [
            moved[m] * -1.0 if m >= len(r) else (r[m] if moved[m] is None else r[m] - moved[m])
            for m in range(len(moved))
        ]
        p = [r[m] + b[k] * p[m] if m < len(p) else r[m] for m in range(len(r))]
        x = [x[m] + a[k + 1] * p[m] if m < len(x) else a[k + 1] * p[m] for m in range(len(p))]
    return x


def shifted(pair):
    lane = iota(1)
    right = [roll(p, -1) for p in pair]
    left = [roll(p, 1) for p in pair]
    right[0] = jnp.where(lane == 127, right[1], right[0])
    left[1] = jnp.where(lane == 0, left[0], left[1])
    return right, left


def edges(strip, zp_count, step, u, r):
    group = step * (BLOCK // zp_count) + u // zp_count
    return roll(strip[u % zp_count, r:r + 8], 120 - 16 * group)


def tree(hi, lo):
    for shift in (4, 2, 1):
        hi, lo = pair_add((hi, lo), (pltpu.roll(hi, shift, 0), pltpu.roll(lo, shift, 0)))
    return hi, lo


def gather(nz, gx, gy, lp_ref, src_ref, v0, tx, ty, tz, tym, yp, ym, q,
           lp, w, s_own, s_left, s_right, to_right, to_left, ws, txs, tys, tzs, b0, b1, b2, b3, fzs,
           load_sem, x_send, x_recv, s_send, s_recv):
    i = lax.axis_index("gx")
    j = lax.axis_index("gy")
    zp_count = nz // 8
    strips = (b0, b1, b2, b3)
    lane, sub = iota(1), iota(0)
    l16, l8 = lane % 16, lane % 8

    def inside(di, dj):
        ok = None
        for cond in (
            [] if di == 0 else [i < gx - 1] if di > 0 else [i > 0]
        ) + ([] if dj == 0 else [j < gy - 1] if dj > 0 else [j > 0]):
            ok = cond if ok is None else jnp.logical_and(ok, cond)
        return ok

    loads = []
    for n, (source, target) in enumerate(((src_ref, v0), (lp_ref, lp))):
        for h in range(2):
            copy = pltpu.make_async_copy(
                source.at[0, :, :, pl.ds(128 * h, 128)],
                target.at[h, :, pl.ds(TOP, 32), :],
                load_sem.at[2 * n + h],
            )
            copy.start()
            loads.append(copy)

    barrier = pltpu.get_barrier_semaphore()
    for di, dj in DIRS:
        @pl.when(inside(di, dj))
        def _():
            pl.semaphore_signal(barrier, inc=1, device_id=(i + di, j + dj), device_id_type=MESH)

    zero4 = jnp.zeros((4, 128), F32)

    @pl.when(i == 0)
    def _():
        def fill(z, carry):
            for h in range(2):
                v0[h, z, 4:8] = zero4
                lp[h, z, 4:8] = zero4
            return carry
        lax.fori_loop(0, nz, fill, 0)
        for buf in (s_own, s_left, s_right):
            for zp in range(buf.shape[0]):
                buf[zp, 4:8] = zero4

    @pl.when(i == gx - 1)
    def _():
        def fill(z, carry):
            for h in range(2):
                v0[h, z, 40:44] = zero4
                lp[h, z, 40:44] = zero4
            return carry
        lax.fori_loop(0, nz, fill, 0)
        for buf in (s_own, s_left, s_right):
            for zp in range(buf.shape[0]):
                buf[zp, 40:44] = zero4

    for edge, buf in ((j == 0, s_left), (j == gy - 1, s_right)):
        @pl.when(edge)
        def _():
            for zp in range(zp_count // 2):
                buf[zp, 4:8] = zero4
                buf[zp, 40:44] = zero4
                for r in OWN:
                    buf[zp, r:r + 8] = jnp.zeros((8, 128), F32)

    inner_i = (i > 0).astype(jnp.int32) + (i < gx - 1).astype(jnp.int32)
    inner_j = (j > 0).astype(jnp.int32) + (j < gy - 1).astype(jnp.int32)
    pl.semaphore_wait(barrier, inner_i + inner_j + inner_i * inner_j)

    x_copies = []
    for step, first, land in ((1, 28, 4), (-1, 0, 40)):
        group = []
        for n, (source, target) in enumerate(((lp_ref, lp), (src_ref, v0))):
            for h in range(2):
                slot = (0 if step > 0 else 4) + 2 * n + h
                group.append(pltpu.make_async_remote_copy(
                    src_ref=source.at[0, :, pl.ds(first, 4), pl.ds(128 * h, 128)],
                    dst_ref=target.at[h, :, pl.ds(land, 4), :],
                    send_sem=x_send.at[slot],
                    recv_sem=x_recv.at[slot],
                    device_id=(i + step, j),
                    device_id_type=MESH,
                ))
        x_copies.append((step, group))

        @pl.when(inside(step, 0))
        def _():
            for copy in group:
                copy.start()

    for copy in loads:
        copy.wait()

    def pack(pair, carry):
        for r in OWN:
            planes = []
            for u in range(2):
                packed = jnp.zeros((8, 128), F32)
                for g in range(8):
                    z = g * zp_count + 2 * pair + u
                    fld = jnp.where(lane < 64, v0[0, z, r:r + 8], v0[1, z, r:r + 8])
                    log = jnp.where(lane < 64, lp[0, z, r:r + 8], lp[1, z, r:r + 8])
                    both = jnp.where(l16 < 8, roll(log, 16 * g + 4), roll(fld, 16 * g + 12))
                    packed = jnp.where(lane // 16 == g, both, packed)
                s_own[2 * pair + u, r:r + 8] = packed
                planes.append(packed)
            to_right[pair, r:r + 8] = jnp.where(l8 < 4, planes[0], roll(planes[1], 4))
            to_left[pair, r:r + 8] = jnp.where(l8 < 4, roll(planes[1], -4), planes[0])
        return carry

    lax.fori_loop(0, zp_count // 2, pack, 0)

    s_copies = []
    for n, (di, dj) in enumerate(DIRS):
        base = s_own if dj == 0 else to_right if dj > 0 else to_left
        target = s_own if dj == 0 else s_left if dj > 0 else s_right
        if di == 0:
            first, land, count = 8, 8, 32
        elif di > 0:
            first, land, count = 36, 4, 4
        else:
            first, land, count = 8, 40, 4
        copy = pltpu.make_async_remote_copy(
            src_ref=base.at[:, pl.ds(first, count), :],
            dst_ref=target.at[:, pl.ds(land, count), :],
            send_sem=s_send.at[n],
            recv_sem=s_recv.at[n],
            device_id=(i + di, j + dj),
            device_id_type=MESH,
        )
        s_copies.append((di, dj, copy))

    for di, dj, copy in s_copies[4:] + s_copies[:4]:
        @pl.when(inside(di, dj))
        def _():
            copy.start()

    def invert(step, carry):
        for u in range(BLOCK):
            for h in range(2):
                for r in OWN:
                    z = BLOCK * step + u
                    w[h, z, r:r + 8] = jnp.exp(-lp[h, z, r:r + 8])
        return carry

    lax.fori_loop(0, nz // BLOCK, invert, 0)

    def faces(step, carry):
        for u in range(BLOCK):
            z = BLOCK * step + u
            above = jnp.minimum(z + 1, nz - 1)
            top = jnp.where(z < nz - 1, 2.0, 0.0)
            for r in OWN:
                mids = [w[h, z, r:r + 8] for h in range(2)]
                right, left = shifted(mids)
                more, less = shifted([v0[h, z, r:r + 8] for h in range(2)])
                for h, mid in enumerate(mids):
                    ty[h, z, r:r + 8] = 2.0 / (mid + right[h])
                    tym[h, z, r:r + 8] = 2.0 / (mid + left[h])
                    tx[h, z, r:r + 8] = 2.0 / (mid + w[h, z, r + 1:r + 9])
                    tz[h, z, r:r + 8] = top / (mid + w[h, above, r:r + 8])
                    yp[h, z, r:r + 8] = more[h]
                    ym[h, z, r:r + 8] = less[h]
        return carry

    lax.fori_loop(0, nz // BLOCK, faces, 0)

    for step, group in x_copies:
        @pl.when(inside(-step, 0))
        def _():
            for copy in group[:2]:
                copy.wait_recv()

    def invert_rim(step, carry):
        for u in range(BLOCK):
            z = BLOCK * step + u
            for h in range(2):
                both = jnp.exp(-jnp.where(sub < 4, lp[h, z, 4:12], lp[h, z, 36:44]))
                w[h, z, 4:8] = both[0:4]
                w[h, z, 40:44] = both[4:8]
        return carry

    lax.fori_loop(0, nz // BLOCK, invert_rim, 0)

    def faces_rim(step, carry):
        layers = []
        for u in range(BLOCK):
            z = BLOCK * step + u
            mids = [jnp.where(sub < 4, w[h, z, 4:12], w[h, z, 35:43]) for h in range(2)]
            layers.append((z, mids, shifted(mids)))
        for z, mids, (right, left) in layers:
            above = jnp.minimum(z + 1, nz - 1)
            top = jnp.where(z < nz - 1, 2.0, 0.0)
            for h, mid in enumerate(mids):
                across = jnp.where(sub < 4, w[h, z, 5:13], w[h, z, 36:44])
                higher = jnp.where(sub < 4, w[h, above, 4:12], w[h, above, 35:43])
                for ref, value in (
                    (tx, 2.0 / (mid + across)),
                    (ty, 2.0 / (mid + right[h])),
                    (tym, 2.0 / (mid + left[h])),
                    (tz, top / (mid + higher)),
                ):
                    ref[h, z, 4:8] = value[0:4]
                    ref[h, z, 39:43] = value[4:8]
        return carry

    lax.fori_loop(0, nz // BLOCK, faces_rim, 0)

    for step, group in x_copies:
        @pl.when(inside(-step, 0))
        def _():
            for copy in group[2:]:
                copy.wait_recv()

    def moved_rim(step, carry):
        layers = []
        for u in range(BLOCK):
            z = BLOCK * step + u
            layers.append((z, shifted([jnp.where(sub < 4, v0[h, z, 4:12], v0[h, z, 36:44]) for h in range(2)])))
        for z, (more, less) in layers:
            for h in range(2):
                for ref, value in ((yp, more[h]), (ym, less[h])):
                    ref[h, z, 4:8] = value[0:4]
                    ref[h, z, 40:44] = value[4:8]
        return carry

    lax.fori_loop(0, nz // BLOCK, moved_rim, 0)

    for di, dj, copy in s_copies:
        @pl.when(inside(-di, -dj))
        def _():
            copy.wait_recv()

    for zp in range(zp_count):
        for r in WIDE:
            own, left, right = s_own[zp, r:r + 8], s_left[zp // 2, r:r + 8], s_right[zp // 2, r:r + 8]
            if zp % 2:
                left, right = roll(left, -4), roll(right, 4)
            moved = roll(jnp.where(l16 < 12, left, own), -8)
            b0[zp, r:r + 8] = jnp.where(l16 < 8, moved, jnp.where(l16 < 12, own, right))
            moved = roll(jnp.where(l16 < 4, own, right), 8)
            log = jnp.where(l16 < 8, jnp.where(l16 < 4, left, own), moved)
            ws[zp, r:r + 8] = jnp.exp(-log)
    for zp in range(zp_count):
        for r in WIDE:
            mid = ws[zp, r:r + 8]
            txs[zp, r:r + 8] = 2.0 / (mid + ws[zp, r + 1:r + 9])
            tys[zp, r:r + 8] = 2.0 / (mid + roll(mid, -1))
            if zp < zp_count - 1:
                tzs[zp, r:r + 8] = 2.0 / (mid + ws[zp + 1, r:r + 8])
            else:
                tzs[zp, r:r + 8] = jnp.where(lane < 112, 2.0 / (mid + roll(ws[0, r:r + 8], -16)), 0.0)
    keep_cols = jnp.logical_and(jnp.logical_or(l16 >= 4, j > 0), jnp.logical_or(l16 < 12, j < gy - 1))
    keep_top = jnp.logical_or(sub >= 4, i > 0)
    keep_bottom = jnp.logical_or(sub < 4, i < gx - 1)
    for k in range(4):
        field = strips[k]
        if k < 3:
            for zp in range(zp_count):
                for r in WIDE:
                    mid = field[zp, r:r + 8]
                    above = field[zp + 1, r:r + 8] if zp < zp_count - 1 else roll(field[0, r:r + 8], -16)
                    fzs[zp, r:r + 8] = tzs[zp, r:r + 8] * (mid - above)
        for zp in range(zp_count):
            for r in WIDE:
                mid = field[zp, r:r + 8]
                fy = tys[zp, r:r + 8] * (mid - roll(mid, -1))
                q[k, zp, r:r + 8] = jnp.where(l16 == 8, roll(fy, 5), roll(fy, -4))
                if k == 3:
                    work = fy * (mid - roll(mid, -1))
                    q[4, zp, r:r + 8] = jnp.where(l16 == 8, roll(work, 5), roll(work, -4))
                    continue
                below = fzs[zp - 1, r:r + 8] if zp else roll(fzs[zp_count - 1, r:r + 8], 16)
                total = txs[zp, r:r + 8] * (mid - field[zp, r + 1:r + 9])
                total = total + txs[zp, r - 1:r + 7] * (mid - field[zp, r - 1:r + 7])
                total = total + (fy - roll(fy, 1)) + (fzs[zp, r:r + 8] - below)
                keep = keep_cols
                if r == 4:
                    keep = jnp.logical_and(keep, keep_top)
                if r == 36:
                    keep = jnp.logical_and(keep, keep_bottom)
                strips[k + 1][zp, r:r + 8] = jnp.where(keep, total, 0.0)

    for di, dj, copy in s_copies:
        @pl.when(inside(di, dj))
        def _():
            copy.wait_send()
    for step, group in x_copies:
        @pl.when(inside(step, 0))
        def _():
            for copy in group:
                copy.wait_send()


def powers(nz, gx, gy, v0, tx, ty, tz, tym, yp0, ym0, q, v1, v2, v3, v4, coef,
           yp1, ym1, yp2, ym2, sides, send_row, red_a, red_b, a_send, a_recv, c_send, c_recv):
    i = lax.axis_index("gx")
    j = lax.axis_index("gy")
    zp_count = nz // 8
    fields = (v0, v1, v2, v3, v4)
    lane, sub = iota(1), iota(0)
    keep_top = jnp.logical_or(sub >= 4, i > 0)
    keep_bottom = jnp.logical_or(sub < 4, i < gx - 1)

    barrier = pltpu.get_barrier_semaphore()

    def greet():
        for d in range(1, gx):
            pl.semaphore_signal(barrier, inc=1, device_id=(lax.rem(i + d, gx), j), device_id_type=MESH)
        for d in range(1, gy):
            pl.semaphore_signal(barrier, inc=1, device_id=(i, lax.rem(j + d, gy)), device_id_type=MESH)

    for n, red in ((gx, red_a), (gy, red_b)):
        for r in range(n, red.shape[0]):
            red[r:r + 1, :] = jnp.zeros((1, 128), F32)


    steps = nz // BLOCK

    def turned(k, step, u, r):
        return edges(q.at[k], zp_count, step, u, r)

    row = jnp.zeros((8, 128), F32)
    found = 0
    for k in range(3):
        src, dst, tiles = fields[k], fields[k + 1], WIDE
        for u in range(BLOCK):
            for n, r in enumerate(tiles):
                sides[0, u, n] = turned(k, 0, u, r)

        def spread(z, dst=dst):
            return [shifted([dst[h, z, r:r + 8] for h in range(2)]) for r in WIDE]

        def settle(z, moved, k=k):
            yp, ym = (yp2, ym2) if k == 1 else (yp1, ym1)
            for r, (right, left) in zip(WIDE, moved):
                for h in range(2):
                    yp[h, z, r:r + 8] = right[h]
                    if k < 2:
                        ym[h, z, r:r + 8] = left[h]

        def block(step, carry, k=k, src=src, dst=dst, tiles=tiles, spread=spread, settle=settle):
            sums, below = list(carry[0]), list(carry[1])
            after, before = ((yp0, ym0), (yp1, ym1), (yp2, ym2))[k]
            now = lax.rem(step, 2)
            coming = jnp.minimum(step + 1, steps - 1)
            moved = {}
            for u in range(BLOCK):
                z = BLOCK * step + u
                last = jnp.maximum(z - BLOCK, u)
                moved = spread(last)
                fresh = [turned(k, coming, u, r) for r in tiles]
                above = jnp.minimum(z + 1, nz - 1)
                for n, r in enumerate(tiles):
                    rows, up, down = slice(r, r + 8), slice(r + 1, r + 9), slice(r - 1, r + 7)
                    side = sides[now, u, n]
                    for h in range(2):
                        v = src[h, z, rows]
                        ahead = ty[h, z, rows] * (v - after[h, z, rows])
                        back = tym[h, z, rows] * (v - before[h, z, rows])
                        if h == 0:
                            back = jnp.where(lane == 0, -side, back)
                        else:
                            ahead = jnp.where(lane == 127, side, ahead)
                        fz = tz[h, z, rows] * (v - src[h, above, rows])
                        total = tx[h, z, rows] * (v - src[h, z, up])
                        total = total + tx[h, z, down] * (v - src[h, z, down])
                        total = total + (ahead + back) + (fz - below[2 * n + h])
                        below[2 * n + h] = fz
                        mine, new = v, total
                        if r == 4:
                            total = jnp.where(keep_top, total, 0.0)
                            mine = jnp.where(sub >= 4, mine, 0.0)
                            new = jnp.where(sub >= 4, total, 0.0)
                        if r == 36:
                            total = jnp.where(keep_bottom, total, 0.0)
                            mine = jnp.where(sub < 4, mine, 0.0)
                            new = jnp.where(sub < 4, total, 0.0)
                        dst[h, z, rows] = total
                        if k == 0:
                            sums[2] = sums[2] + mine * mine
                        sums[0] = sums[0] + mine * new
                        sums[1] = sums[1] + new * new
                for n in range(len(tiles)):
                    sides[1 - now, u, n] = fresh[n]
                settle(last, moved)
            return tuple(sums), tuple(below)

        zero = jnp.zeros((8, 128), F32)
        count = 2 if k else 3
        sums, _ = lax.fori_loop(0, steps, block, ((zero,) * count, (zero,) * (2 * len(tiles))))
        for u in range(BLOCK):
            settle(nz - BLOCK + u, spread(nz - BLOCK + u))
        if k == 0:
            greet()
        for part in ([sums[2]] if k == 0 else []) + list(sums[:2]):
            row = jnp.where(lane == found, jnp.sum(part, axis=1, keepdims=True), row)
            found += 1

    for u in range(BLOCK):
        for n, r in enumerate(OWN):
            sides[0, u, n] = turned(4, 0, u, r)
    first_row = jnp.logical_and(sub == 0, i == 0)
    first_col = jnp.logical_and(lane == 0, j == 0)

    def energy(step, carry):
        acc = list(carry)
        now = lax.rem(step, 2)
        coming = jnp.minimum(step + 1, steps - 1)
        for u in range(BLOCK):
            z = BLOCK * step + u
            fresh = [turned(4, coming, u, r) for r in OWN]
            above = jnp.minimum(z + 1, nz - 1)
            for n, r in enumerate(OWN):
                rows, up, down = slice(r, r + 8), slice(r + 1, r + 9), slice(r - 1, r + 7)
                side = sides[now, u, n]
                for h in range(2):
                    v = v3[h, z, rows]
                    dx, dy, dz = v - v3[h, z, up], v - yp1[h, z, rows], v - v3[h, above, rows]
                    across = ty[h, z, rows] * dy * dy
                    if h == 0:
                        acc[n] = acc[n] + jnp.where(first_col, side, 0.0)
                    else:
                        across = jnp.where(lane == 127, side, across)
                    if r == OWN[0]:
                        dm = v - v3[h, z, down]
                        acc[h + 1] = acc[h + 1] + jnp.where(first_row, tx[h, z, down] * dm * dm, 0.0)
                    term = tx[h, z, rows] * dx * dx + (across + tz[h, z, rows] * dz * dz)
                    acc[4 * h + n] = acc[4 * h + n] + term
            for n in range(len(OWN)):
                sides[1 - now, u, n] = fresh[n]
        return tuple(acc)

    zero = jnp.zeros((8, 128), F32)
    acc = lax.fori_loop(0, steps, energy, (zero,) * 8)
    part = ((acc[0] + acc[1]) + (acc[2] + acc[3])) + ((acc[4] + acc[5]) + (acc[6] + acc[7]))
    row = jnp.where(lane == found, jnp.sum(part, axis=1, keepdims=True), row)
    row = jnp.sum(row, axis=0, keepdims=True)

    def fourth():
        def block(step, below):
            below, shifts = list(below), {}
            for u in range(BLOCK):
                z = BLOCK * step + u
                for n, r in enumerate(OWN):
                    left = [roll(v3[h, z, r:r + 8], 1) for h in range(2)]
                    shifts[u, n] = (left[0], jnp.where(lane == 0, left[0], left[1]), turned(3, step, u, r))
            for u in range(BLOCK):
                z = BLOCK * step + u
                above = jnp.minimum(z + 1, nz - 1)
                for n, r in enumerate(OWN):
                    rows, up, down = slice(r, r + 8), slice(r + 1, r + 9), slice(r - 1, r + 7)
                    side = shifts[u, n][2]
                    for h in range(2):
                        v = v3[h, z, rows]
                        ahead = ty[h, z, rows] * (v - yp1[h, z, rows])
                        back = tym[h, z, rows] * (v - shifts[u, n][h])
                        if h == 0:
                            back = jnp.where(lane == 0, -side, back)
                        else:
                            ahead = jnp.where(lane == 127, side, ahead)
                        fz = tz[h, z, rows] * (v - v3[h, above, rows])
                        total = tx[h, z, rows] * (v - v3[h, z, up])
                        total = total + tx[h, z, down] * (v - v3[h, z, down])
                        v4[h, z, rows] = total + (ahead + back) + (fz - below[2 * n + h])
                        below[2 * n + h] = fz
            return tuple(below)

        lax.fori_loop(0, steps, block, (zero,) * (2 * len(OWN)))


    def exchange(value, slot, red, count, send, recv, where, meanwhile=None):
        send_row[slot:slot + 1, :] = value
        red[0:1, :] = value
        copies = []
        far = (lambda d: -min(d, count - d)) if count == gx else (
            lambda d: -min(d % 4, 4 - d % 4) - min(d // 4, 4 - d // 4))
        for d in sorted(range(1, count), key=far):
            copies.append(pltpu.make_async_remote_copy(
                src_ref=send_row.at[pl.ds(slot, 1), :],
                dst_ref=red.at[pl.ds(count - d, 1), :],
                send_sem=send.at[d],
                recv_sem=recv.at[count - d],
                device_id=where(d),
                device_id_type=MESH,
            ))
        for copy in copies:
            copy.start()
        if meanwhile is not None:
            meanwhile()
        for copy in copies:
            copy.wait_recv()
        return copies

    pl.semaphore_wait(barrier, gx - 1 + gy - 1)
    sent = exchange(row, 0, red_a, gx, a_send, a_recv, lambda d: (lax.rem(i + d, gx), j), fourth)
    part = red_a[...]
    hi, lo = tree(part, jnp.zeros_like(part))
    row = jnp.where(lane < 8, hi, pltpu.roll(lo, 8, 1))[0:1]
    sent += exchange(row, 8, red_b, gy, c_send, c_recv, lambda d: (i, lax.rem(j + d, gy)))
    parts = []
    for r in range(0, red_b.shape[0], 8):
        part = red_b[r:r + 8]
        parts.append((part, pltpu.roll(part, 120, 1)))
    total = parts[0]
    for part in parts[1:]:
        total = pair_add(total, part)
    hi, lo = tree(*total)
    splat = [
        (jnp.broadcast_to(hi[:, n:n + 1], (8, 128)), jnp.broadcast_to(lo[:, n:n + 1], (8, 128)))
        for n in range(8)
    ]
    for n, value in enumerate(coefficients(splat)):
        coef[n] = value

    for copy in sent:
        copy.wait_send()


def finish(nz, v0, v1, v2, v3, v4, tx, ty, q, coef, p_out, r_out, e_out, n_out,
           p_buf, r_buf, e_buf, n_buf, wide, side, sems):
    zp_count = nz // 8
    chunk = nz // PARTS
    lane = iota(1)
    c = [coef[n] for n in range(4)]

    def combine(parts):
        return (c[0] * parts[0] + c[1] * parts[1]) + (c[2] * parts[2] + c[3] * parts[3])

    for zp in range(zp_count):
        for r in OWN:
            side[zp, r:r + 8] = combine([q[k, zp, r:r + 8] for k in range(4)])

    def block(step, carry):
        moved = {}

        def first(u):
            z = BLOCK * step + u
            for r in OWN:
                press = []
                for h in range(2):
                    v = [f[h, z, r:r + 8] for f in (v0, v1, v2, v3)]
                    press.append(combine(v))
                    wide[u, h, r:r + 8] = press[h]
                    cols = slice(128 * h, 128 * h + 128)
                    p_buf[z, r - 8:r, cols] = press[h]
                    r_buf[z, r - 8:r, cols] = v[0] - combine(v[1:] + [v4[h, z, r:r + 8]])
                moved[u, r] = [roll(p, -1) for p in press]
                moved[u, r].append(edges(side, zp_count, step, u, r))
            for h in range(2):
                wide[u, h, 40:48] = combine([f[h, z, 40:48] for f in (v0, v1, v2, v3)])

        def second(u):
            z = BLOCK * step + u
            for r in OWN:
                one, two, rim = moved[u, r]
                for h, across in ((0, jnp.where(lane == 127, two, one)), (1, two)):
                    cols = slice(128 * h, 128 * h + 128)
                    press = wide[u, h, r:r + 8]
                    e_buf[z, r - 8:r, cols] = tx[h, z, r:r + 8] * (press - wide[u, h, r + 1:r + 9])
                    north = ty[h, z, r:r + 8] * (press - across)
                    if h == 1:
                        north = jnp.where(lane == 127, rim, north)
                    n_buf[z, r - 8:r, cols] = north

        for u in range(BLOCK):
            first(u)
            if u:
                second(u - 1)
        second(BLOCK - 1)
        return carry

    copies = []
    for part in range(PARTS):
        lax.fori_loop(part * chunk // BLOCK, (part + 1) * chunk // BLOCK, block, 0)
        for n, (buf, out) in enumerate(((p_buf, p_out), (r_buf, r_out), (e_buf, e_out), (n_buf, n_out))):
            copy = pltpu.make_async_copy(
                buf.at[pl.ds(part * chunk, chunk)],
                out.at[0, pl.ds(part * chunk, chunk)],
                sems.at[4 * part + n],
            )
            copy.start()
            copies.append(copy)
    for copy in copies:
        copy.wait()


def solution(mesh):
    gx, gy = mesh.shape["gx"], mesh.shape["gy"]

    def on_device(log_perm, source):
        nz = log_perm.shape[1]
        zp = nz // 8
        field = (2, nz, ROWS, 128)
        strip = (zp, ROWS, 128)
        vmem = pl.BlockSpec(memory_space=pltpu.VMEM)
        hbm = pl.BlockSpec(memory_space=pltpu.HBM)
        made = pl.pallas_call(
            functools.partial(gather, nz, gx, gy),
            out_shape=[pltpu.VMEM(field, F32)] * 7 + [pltpu.VMEM((5,) + strip, F32)],
            in_specs=[hbm] * 2,
            out_specs=[vmem] * 8,
            scratch_shapes=[pltpu.VMEM(field, F32)] * 2
            + [pltpu.VMEM(strip, F32)]
            + [pltpu.VMEM((zp // 2, ROWS, 128), F32)] * 4
            + [pltpu.VMEM(strip, F32)] * 9
            + [pltpu.SemaphoreType.DMA((4,))]
            + [pltpu.SemaphoreType.DMA((8,))] * 4,
            compiler_params=pltpu.CompilerParams(
                collective_id=0, has_side_effects=True, vmem_limit_bytes=16 << 20
            ),
            name="gather",
        )(*(pltpu.with_memory_space_constraint(x, pltpu.HBM) for x in (log_perm, source)))
        v0, tx, ty, tz, tym, yp, ym, q = made
        v1, v2, v3, v4, coef = pl.pallas_call(
            functools.partial(powers, nz, gx, gy),
            out_shape=[pltpu.VMEM(field, F32)] * 4 + [pltpu.VMEM((4, 8, 128), F32)],
            in_specs=[vmem] * 8,
            out_specs=[vmem] * 5,
            scratch_shapes=[pltpu.VMEM(field, F32)] * 4
            + [
                pltpu.VMEM((2, BLOCK, 5, 8, 128), F32),
                pltpu.VMEM((16, 128), F32),
                pltpu.VMEM((8, 128), F32),
                pltpu.VMEM((max(8, gy), 128), F32),
            ]
            + [pltpu.SemaphoreType.DMA((gx,))] * 2
            + [pltpu.SemaphoreType.DMA((gy,))] * 2,
            compiler_params=pltpu.CompilerParams(
                collective_id=1, has_side_effects=True, vmem_limit_bytes=14 << 20
            ),
            name="powers",
        )(*made)
        shape = jax.ShapeDtypeStruct(log_perm.shape, F32)
        return pl.pallas_call(
            functools.partial(finish, nz),
            out_shape=[shape] * 4,
            in_specs=[vmem] * 9,
            out_specs=[hbm] * 4,
            scratch_shapes=[pltpu.VMEM((nz, 32, 256), F32)] * 4
            + [pltpu.VMEM((BLOCK, 2, ROWS, 128), F32), pltpu.VMEM(strip, F32), pltpu.SemaphoreType.DMA((4 * PARTS,))],
            compiler_params=pltpu.CompilerParams(vmem_limit_bytes=12 << 20),
            name="finish",
        )(v0, v1, v2, v3, v4, tx, ty, q, coef)

    spec = P(None, None, "gx", "gy")
    return jax.shard_map(
        on_device, mesh=mesh, in_specs=(spec, spec), out_specs=(spec,) * 4, check_vma=False
    )
```

```python
import functools

import jax
import jax.numpy as jnp
from jax import lax
from jax.experimental import pallas as pl
from jax.experimental.pallas import tpu as pltpu
from jax.sharding import PartitionSpec as P

MESH = pl.DeviceIdType.MESH
F32 = jnp.float32
TOP = 8
ROWS = 48
WIDE = (4, 12, 20, 28, 36)
OWN = (8, 16, 24, 32)
PARTS = 4
BLOCK = 8
DIRS = ((0, 1), (0, -1), (1, 0), (-1, 0), (1, 1), (1, -1), (-1, 1), (-1, -1))


def iota(dim):
    return lax.broadcasted_iota(jnp.int32, (8, 128), dim)


def roll(value, amount):
    return pltpu.roll(value, amount % 128 if isinstance(amount, int) else amount, 1)


def two_sum(a, b):
    s = a + b
    t = s - a
    return s, (a - (s - t)) + (b - t)


def quick(a, b):
    s = a + b
    return s, b - (s - a)


def pair_add(x, y):
    s, e = two_sum(x[0], y[0])
    return quick(s, e + (x[1] + y[1]))


def halves(a):
    t = a * 4097.0
    hi = t - (t - a)
    return hi, a - hi


def pair_mul(x, y):
    p = x[0] * y[0]
    xh, xl = halves(x[0])
    yh, yl = halves(y[0])
    e = ((xh * yh - p) + xh * yl + xl * yh) + xl * yl
    return quick(p, e + (x[0] * y[1] + x[1] * y[0]))


def neg(x):
    return (-x[0], -x[1])


def pair_div(x, y):
    q = x[0] / y[0]
    p = q * y[0]
    qh, ql = halves(q)
    yh, yl = halves(y[0])
    e = ((qh * yh - p) + qh * yl + ql * yh) + ql * yl
    rest = ((x[0] - p) - (e + q * y[1])) + x[1]
    return quick(q, rest / y[0])


def coefficients(moments):
    resid, direc = dict(enumerate(moments)), dict(enumerate(moments))
    steps, ratios = [], []
    for k in range(4):
        step = pair_div(resid[k], direc[k + 1])
        steps.append(step)
        if k == 3:
            break
        fresh = {}
        for l in range(k + 1, 7 - k):
            fresh[l] = pair_add(resid[l], neg(pair_mul(step, direc[l + 1])))
        ratio = neg(pair_div(pair_mul(step, fresh[k + 1]), resid[k]))
        ratios.append(ratio)
        direc = {l: pair_add(fresh[l], pair_mul(ratio, direc[l])) for l in fresh}
        resid = fresh
    a = [s[0] for s in steps]
    b = [r[0] for r in ratios]
    one = jnp.ones_like(a[0])
    r, p = [one], [one]
    x = [a[0]]
    for k in range(3):
        moved = [None] + [a[k] * c for c in p]
        r = [
            moved[m] * -1.0 if m >= len(r) else (r[m] if moved[m] is None else r[m] - moved[m])
            for m in range(len(moved))
        ]
        p = [r[m] + b[k] * p[m] if m < len(p) else r[m] for m in range(len(r))]
        x = [x[m] + a[k + 1] * p[m] if m < len(x) else a[k + 1] * p[m] for m in range(len(p))]
    return x


def shifted(pair):
    lane = iota(1)
    right = [roll(p, -1) for p in pair]
    left = [roll(p, 1) for p in pair]
    right[0] = jnp.where(lane == 127, right[1], right[0])
    left[1] = jnp.where(lane == 0, left[0], left[1])
    return right, left


def edges(strip, zp_count, step, u, r):
    group = step * (BLOCK // zp_count) + u // zp_count
    return roll(strip[u % zp_count, r:r + 8], 120 - 16 * group)


def tree(hi, lo):
    for shift in (4, 2, 1):
        hi, lo = pair_add((hi, lo), (pltpu.roll(hi, shift, 0), pltpu.roll(lo, shift, 0)))
    return hi, lo


def gather(nz, gx, gy, lp_ref, src_ref, v0, tx, ty, tz, tym, yp, ym, q,
           lp, w, s_own, s_left, s_right, to_right, to_left, ws, txs, tys, tzs, b0, b1, b2, b3, fzs,
           load_sem, x_send, x_recv, s_send, s_recv):
    i = lax.axis_index("gx")
    j = lax.axis_index("gy")
    zp_count = nz // 8
    strips = (b0, b1, b2, b3)
    lane, sub = iota(1), iota(0)
    l16, l8 = lane % 16, lane % 8

    def inside(di, dj):
        ok = None
        for cond in (
            [] if di == 0 else [i < gx - 1] if di > 0 else [i > 0]
        ) + ([] if dj == 0 else [j < gy - 1] if dj > 0 else [j > 0]):
            ok = cond if ok is None else jnp.logical_and(ok, cond)
        return ok

    loads = []
    for n, (source, target) in enumerate(((src_ref, v0), (lp_ref, lp))):
        for h in range(2):
            copy = pltpu.make_async_copy(
                source.at[0, :, :, pl.ds(128 * h, 128)],
                target.at[h, :, pl.ds(TOP, 32), :],
                load_sem.at[2 * n + h],
            )
            copy.start()
            loads.append(copy)

    barrier = pltpu.get_barrier_semaphore()
    for di, dj in DIRS:
        @pl.when(inside(di, dj))
        def _():
            pl.semaphore_signal(barrier, inc=1, device_id=(i + di, j + dj), device_id_type=MESH)

    zero4 = jnp.zeros((4, 128), F32)

    @pl.when(i == 0)
    def _():
        def fill(z, carry):
            for h in range(2):
                v0[h, z, 4:8] = zero4
                lp[h, z, 4:8] = zero4
            return carry
        lax.fori_loop(0, nz, fill, 0)
        for buf in (s_own, s_left, s_right):
            for zp in range(buf.shape[0]):
                buf[zp, 4:8] = zero4

    @pl.when(i == gx - 1)
    def _():
        def fill(z, carry):
            for h in range(2):
                v0[h, z, 40:44] = zero4
                lp[h, z, 40:44] = zero4
            return carry
        lax.fori_loop(0, nz, fill, 0)
        for buf in (s_own, s_left, s_right):
            for zp in range(buf.shape[0]):
                buf[zp, 40:44] = zero4

    for edge, buf in ((j == 0, s_left), (j == gy - 1, s_right)):
        @pl.when(edge)
        def _():
            for zp in range(zp_count // 2):
                buf[zp, 4:8] = zero4
                buf[zp, 40:44] = zero4
                for r in OWN:
                    buf[zp, r:r + 8] = jnp.zeros((8, 128), F32)

    inner_i = (i > 0).astype(jnp.int32) + (i < gx - 1).astype(jnp.int32)
    inner_j = (j > 0).astype(jnp.int32) + (j < gy - 1).astype(jnp.int32)
    pl.semaphore_wait(barrier, inner_i + inner_j + inner_i * inner_j)

    x_copies = []
    for step, first, land in ((1, 28, 4), (-1, 0, 40)):
        group = []
        for n, (source, target) in enumerate(((lp_ref, lp), (src_ref, v0))):
            for h in range(2):
                slot = (0 if step > 0 else 4) + 2 * n + h
                group.append(pltpu.make_async_remote_copy(
                    src_ref=source.at[0, :, pl.ds(first, 4), pl.ds(128 * h, 128)],
                    dst_ref=target.at[h, :, pl.ds(land, 4), :],
                    send_sem=x_send.at[slot],
                    recv_sem=x_recv.at[slot],
                    device_id=(i + step, j),
                    device_id_type=MESH,
                ))
        x_copies.append((step, group))

        @pl.when(inside(step, 0))
        def _():
            for copy in group:
                copy.start()

    for copy in loads:
        copy.wait()

    def pack(pair, carry):
        for r in OWN:
            planes = []
            for u in range(2):
                packed = jnp.zeros((8, 128), F32)
                for g in range(8):
                    z = g * zp_count + 2 * pair + u
                    fld = jnp.where(lane < 64, v0[0, z, r:r + 8], v0[1, z, r:r + 8])
                    log = jnp.where(lane < 64, lp[0, z, r:r + 8], lp[1, z, r:r + 8])
                    both = jnp.where(l16 < 8, roll(log, 16 * g + 4), roll(fld, 16 * g + 12))
                    packed = jnp.where(lane // 16 == g, both, packed)
                s_own[2 * pair + u, r:r + 8] = packed
                planes.append(packed)
            to_right[pair, r:r + 8] = jnp.where(l8 < 4, planes[0], roll(planes[1], 4))
            to_left[pair, r:r + 8] = jnp.where(l8 < 4, roll(planes[1], -4), planes[0])
        return carry

    lax.fori_loop(0, zp_count // 2, pack, 0)

    s_copies = []
    for n, (di, dj) in enumerate(DIRS):
        base = s_own if dj == 0 else to_right if dj > 0 else to_left
        target = s_own if dj == 0 else s_left if dj > 0 else s_right
        if di == 0:
            first, land, count = 8, 8, 32
        elif di > 0:
            first, land, count = 36, 4, 4
        else:
            first, land, count = 8, 40, 4
        copy = pltpu.make_async_remote_copy(
            src_ref=base.at[:, pl.ds(first, count), :],
            dst_ref=target.at[:, pl.ds(land, count), :],
            send_sem=s_send.at[n],
            recv_sem=s_recv.at[n],
            device_id=(i + di, j + dj),
            device_id_type=MESH,
        )
        s_copies.append((di, dj, copy))

    for di, dj, copy in s_copies[4:] + s_copies[:4]:
        @pl.when(inside(di, dj))
        def _():
            copy.start()

    def invert(step, carry):
        for u in range(BLOCK):
            for h in range(2):
                for r in OWN:
                    z = BLOCK * step + u
                    w[h, z, r:r + 8] = jnp.exp(-lp[h, z, r:r + 8])
        return carry

    lax.fori_loop(0, nz // BLOCK, invert, 0)

    def faces(step, carry):
        for u in range(BLOCK):
            z = BLOCK * step + u
            above = jnp.minimum(z + 1, nz - 1)
            top = jnp.where(z < nz - 1, 2.0, 0.0)
            for r in OWN:
                mids = [w[h, z, r:r + 8] for h in range(2)]
                right, left = shifted(mids)
                more, less = shifted([v0[h, z, r:r + 8] for h in range(2)])
                for h, mid in enumerate(mids):
                    ty[h, z, r:r + 8] = 2.0 / (mid + right[h])
                    tym[h, z, r:r + 8] = 2.0 / (mid + left[h])
                    tx[h, z, r:r + 8] = 2.0 / (mid + w[h, z, r + 1:r + 9])
                    tz[h, z, r:r + 8] = top / (mid + w[h, above, r:r + 8])
                    yp[h, z, r:r + 8] = more[h]
                    ym[h, z, r:r + 8] = less[h]
        return carry

    lax.fori_loop(0, nz // BLOCK, faces, 0)

    for step, group in x_copies:
        @pl.when(inside(-step, 0))
        def _():
            for copy in group[:2]:
                copy.wait_recv()

    def invert_rim(step, carry):
        for u in range(BLOCK):
            z = BLOCK * step + u
            for h in range(2):
                both = jnp.exp(-jnp.where(sub < 4, lp[h, z, 4:12], lp[h, z, 36:44]))
                w[h, z, 4:8] = both[0:4]
                w[h, z, 40:44] = both[4:8]
        return carry

    lax.fori_loop(0, nz // BLOCK, invert_rim, 0)

    def faces_rim(step, carry):
        layers = []
        for u in range(BLOCK):
            z = BLOCK * step + u
            mids = [jnp.where(sub < 4, w[h, z, 4:12], w[h, z, 35:43]) for h in range(2)]
            layers.append((z, mids, shifted(mids)))
        for z, mids, (right, left) in layers:
            above = jnp.minimum(z + 1, nz - 1)
            top = jnp.where(z < nz - 1, 2.0, 0.0)
            for h, mid in enumerate(mids):
                across = jnp.where(sub < 4, w[h, z, 5:13], w[h, z, 36:44])
                higher = jnp.where(sub < 4, w[h, above, 4:12], w[h, above, 35:43])
                for ref, value in (
                    (tx, 2.0 / (mid + across)),
                    (ty, 2.0 / (mid + right[h])),
                    (tym, 2.0 / (mid + left[h])),
                    (tz, top / (mid + higher)),
                ):
                    ref[h, z, 4:8] = value[0:4]
                    ref[h, z, 39:43] = value[4:8]
        return carry

    lax.fori_loop(0, nz // BLOCK, faces_rim, 0)

    for step, group in x_copies:
        @pl.when(inside(-step, 0))
        def _():
            for copy in group[2:]:
                copy.wait_recv()

    def moved_rim(step, carry):
        layers = []
        for u in range(BLOCK):
            z = BLOCK * step + u
            layers.append((z, shifted([jnp.where(sub < 4, v0[h, z, 4:12], v0[h, z, 36:44]) for h in range(2)])))
        for z, (more, less) in layers:
            for h in range(2):
                for ref, value in ((yp, more[h]), (ym, less[h])):
                    ref[h, z, 4:8] = value[0:4]
                    ref[h, z, 40:44] = value[4:8]
        return carry

    lax.fori_loop(0, nz // BLOCK, moved_rim, 0)

    for di, dj, copy in s_copies:
        @pl.when(inside(-di, -dj))
        def _():
            copy.wait_recv()

    for zp in range(zp_count):
        for r in WIDE:
            own, left, right = s_own[zp, r:r + 8], s_left[zp // 2, r:r + 8], s_right[zp // 2, r:r + 8]
            if zp % 2:
                left, right = roll(left, -4), roll(right, 4)
            moved = roll(jnp.where(l16 < 12, left, own), -8)
            b0[zp, r:r + 8] = jnp.where(l16 < 8, moved, jnp.where(l16 < 12, own, right))
            moved = roll(jnp.where(l16 < 4, own, right), 8)
            log = jnp.where(l16 < 8, jnp.where(l16 < 4, left, own), moved)
            ws[zp, r:r + 8] = jnp.exp(-log)
    for zp in range(zp_count):
        for r in WIDE:
            mid = ws[zp, r:r + 8]
            txs[zp, r:r + 8] = 2.0 / (mid + ws[zp, r + 1:r + 9])
            tys[zp, r:r + 8] = 2.0 / (mid + roll(mid, -1))
            if zp < zp_count - 1:
                tzs[zp, r:r + 8] = 2.0 / (mid + ws[zp + 1, r:r + 8])
            else:
                tzs[zp, r:r + 8] = jnp.where(lane < 112, 2.0 / (mid + roll(ws[0, r:r + 8], -16)), 0.0)
    keep_cols = jnp.logical_and(jnp.logical_or(l16 >= 4, j > 0), jnp.logical_or(l16 < 12, j < gy - 1))
    keep_top = jnp.logical_or(sub >= 4, i > 0)
    keep_bottom = jnp.logical_or(sub < 4, i < gx - 1)
    for k in range(4):
        field = strips[k]
        if k < 3:
            for zp in range(zp_count):
                for r in WIDE:
                    mid = field[zp, r:r + 8]
                    above = field[zp + 1, r:r + 8] if zp < zp_count - 1 else roll(field[0, r:r + 8], -16)
                    fzs[zp, r:r + 8] = tzs[zp, r:r + 8] * (mid - above)
        for zp in range(zp_count):
            for r in WIDE:
                mid = field[zp, r:r + 8]
                fy = tys[zp, r:r + 8] * (mid - roll(mid, -1))
                q[k, zp, r:r + 8] = jnp.where(l16 == 8, roll(fy, 5), roll(fy, -4))
                if k == 3:
                    work = fy * (mid - roll(mid, -1))
                    q[4, zp, r:r + 8] = jnp.where(l16 == 8, roll(work, 5), roll(work, -4))
                    continue
                below = fzs[zp - 1, r:r + 8] if zp else roll(fzs[zp_count - 1, r:r + 8], 16)
                total = txs[zp, r:r + 8] * (mid - field[zp, r + 1:r + 9])
                total = total + txs[zp, r - 1:r + 7] * (mid - field[zp, r - 1:r + 7])
                total = total + (fy - roll(fy, 1)) + (fzs[zp, r:r + 8] - below)
                keep = keep_cols
                if r == 4:
                    keep = jnp.logical_and(keep, keep_top)
                if r == 36:
                    keep = jnp.logical_and(keep, keep_bottom)
                strips[k + 1][zp, r:r + 8] = jnp.where(keep, total, 0.0)

    for di, dj, copy in s_copies:
        @pl.when(inside(di, dj))
        def _():
            copy.wait_send()
    for step, group in x_copies:
        @pl.when(inside(step, 0))
        def _():
            for copy in group:
                copy.wait_send()


def powers(nz, gx, gy, v0, tx, ty, tz, tym, yp0, ym0, q, v1, v2, v3, v4, coef,
           yp1, ym1, yp2, ym2, sides, send_row, red_a, red_b, a_send, a_recv, c_send, c_recv):
    i = lax.axis_index("gx")
    j = lax.axis_index("gy")
    zp_count = nz // 8
    fields = (v0, v1, v2, v3, v4)
    lane, sub = iota(1), iota(0)
    keep_top = jnp.logical_or(sub >= 4, i > 0)
    keep_bottom = jnp.logical_or(sub < 4, i < gx - 1)

    barrier = pltpu.get_barrier_semaphore()

    def greet():
        for d in range(1, gx):
            pl.semaphore_signal(barrier, inc=1, device_id=(lax.rem(i + d, gx), j), device_id_type=MESH)
        for d in range(1, gy):
            pl.semaphore_signal(barrier, inc=1, device_id=(i, lax.rem(j + d, gy)), device_id_type=MESH)

    for n, red in ((gx, red_a), (gy, red_b)):
        for r in range(n, red.shape[0]):
            red[r:r + 1, :] = jnp.zeros((1, 128), F32)


    steps = nz // BLOCK

    def turned(k, step, u, r):
        return edges(q.at[k], zp_count, step, u, r)

    row = jnp.zeros((8, 128), F32)
    found = 0
    for k in range(3):
        src, dst, tiles = fields[k], fields[k + 1], WIDE
        for u in range(BLOCK):
            for n, r in enumerate(tiles):
                sides[0, u, n] = turned(k, 0, u, r)

        def spread(z, dst=dst):
            return [shifted([dst[h, z, r:r + 8] for h in range(2)]) for r in WIDE]

        def settle(z, moved, k=k):
            yp, ym = (yp2, ym2) if k == 1 else (yp1, ym1)
            for r, (right, left) in zip(WIDE, moved):
                for h in range(2):
                    yp[h, z, r:r + 8] = right[h]
                    if k < 2:
                        ym[h, z, r:r + 8] = left[h]

        def block(step, carry, k=k, src=src, dst=dst, tiles=tiles, spread=spread, settle=settle):
            sums, below = list(carry[0]), list(carry[1])
            after, before = ((yp0, ym0), (yp1, ym1), (yp2, ym2))[k]
            now = lax.rem(step, 2)
            coming = jnp.minimum(step + 1, steps - 1)
            moved = {}
            for u in range(BLOCK):
                z = BLOCK * step + u
                last = jnp.maximum(z - BLOCK, u)
                moved = spread(last)
                fresh = [turned(k, coming, u, r) for r in tiles]
                above = jnp.minimum(z + 1, nz - 1)
                for n, r in enumerate(tiles):
                    rows, up, down = slice(r, r + 8), slice(r + 1, r + 9), slice(r - 1, r + 7)
                    side = sides[now, u, n]
                    for h in range(2):
                        v = src[h, z, rows]
                        ahead = ty[h, z, rows] * (v - after[h, z, rows])
                        back = tym[h, z, rows] * (v - before[h, z, rows])
                        if h == 0:
                            back = jnp.where(lane == 0, -side, back)
                        else:
                            ahead = jnp.where(lane == 127, side, ahead)
                        fz = tz[h, z, rows] * (v - src[h, above, rows])
                        total = tx[h, z, rows] * (v - src[h, z, up])
                        total = total + tx[h, z, down] * (v - src[h, z, down])
                        total = total + (ahead + back) + (fz - below[2 * n + h])
                        below[2 * n + h] = fz
                        mine, new = v, total
                        if r == 4:
                            total = jnp.where(keep_top, total, 0.0)
                            mine = jnp.where(sub >= 4, mine, 0.0)
                            new = jnp.where(sub >= 4, total, 0.0)
                        if r == 36:
                            total = jnp.where(keep_bottom, total, 0.0)
                            mine = jnp.where(sub < 4, mine, 0.0)
                            new = jnp.where(sub < 4, total, 0.0)
                        dst[h, z, rows] = total
                        if k == 0:
                            sums[2] = sums[2] + mine * mine
                        sums[0] = sums[0] + mine * new
                        sums[1] = sums[1] + new * new
                for n in range(len(tiles)):
                    sides[1 - now, u, n] = fresh[n]
                settle(last, moved)
            return tuple(sums), tuple(below)

        zero = jnp.zeros((8, 128), F32)
        count = 2 if k else 3
        sums, _ = lax.fori_loop(0, steps, block, ((zero,) * count, (zero,) * (2 * len(tiles))))
        for u in range(BLOCK):
            settle(nz - BLOCK + u, spread(nz - BLOCK + u))
        if k == 0:
            greet()
        for part in ([sums[2]] if k == 0 else []) + list(sums[:2]):
            row = jnp.where(lane == found, jnp.sum(part, axis=1, keepdims=True), row)
            found += 1

    for u in range(BLOCK):
        for n, r in enumerate(OWN):
            sides[0, u, n] = turned(4, 0, u, r)
    first_row = jnp.logical_and(sub == 0, i == 0)
    first_col = jnp.logical_and(lane == 0, j == 0)

    def energy(step, carry):
        acc = list(carry)
        now = lax.rem(step, 2)
        coming = jnp.minimum(step + 1, steps - 1)
        for u in range(BLOCK):
            z = BLOCK * step + u
            fresh = [turned(4, coming, u, r) for r in OWN]
            above = jnp.minimum(z + 1, nz - 1)
            for n, r in enumerate(OWN):
                rows, up, down = slice(r, r + 8), slice(r + 1, r + 9), slice(r - 1, r + 7)
                side = sides[now, u, n]
                for h in range(2):
                    v = v3[h, z, rows]
                    dx, dy, dz = v - v3[h, z, up], v - yp1[h, z, rows], v - v3[h, above, rows]
                    across = ty[h, z, rows] * dy * dy
                    if h == 0:
                        acc[n] = acc[n] + jnp.where(first_col, side, 0.0)
                    else:
                        across = jnp.where(lane == 127, side, across)
                    if r == OWN[0]:
                        dm = v - v3[h, z, down]
                        acc[h + 1] = acc[h + 1] + jnp.where(first_row, tx[h, z, down] * dm * dm, 0.0)
                    term = tx[h, z, rows] * dx * dx + (across + tz[h, z, rows] * dz * dz)
                    acc[4 * h + n] = acc[4 * h + n] + term
            for n in range(len(OWN)):
                sides[1 - now, u, n] = fresh[n]
        return tuple(acc)

    zero = jnp.zeros((8, 128), F32)
    acc = lax.fori_loop(0, steps, energy, (zero,) * 8)
    part = ((acc[0] + acc[1]) + (acc[2] + acc[3])) + ((acc[4] + acc[5]) + (acc[6] + acc[7]))
    row = jnp.where(lane == found, jnp.sum(part, axis=1, keepdims=True), row)
    row = jnp.sum(row, axis=0, keepdims=True)

    def fourth():
        def block(step, below):
            below, shifts = list(below), {}
            for u in range(BLOCK):
                z = BLOCK * step + u
                for n, r in enumerate(OWN):
                    left = [roll(v3[h, z, r:r + 8], 1) for h in range(2)]
                    shifts[u, n] = (left[0], jnp.where(lane == 0, left[0], left[1]), turned(3, step, u, r))
            for u in range(BLOCK):
                z = BLOCK * step + u
                above = jnp.minimum(z + 1, nz - 1)
                for n, r in enumerate(OWN):
                    rows, up, down = slice(r, r + 8), slice(r + 1, r + 9), slice(r - 1, r + 7)
                    side = shifts[u, n][2]
                    for h in range(2):
                        v = v3[h, z, rows]
                        ahead = ty[h, z, rows] * (v - yp1[h, z, rows])
                        back = tym[h, z, rows] * (v - shifts[u, n][h])
                        if h == 0:
                            back = jnp.where(lane == 0, -side, back)
                        else:
                            ahead = jnp.where(lane == 127, side, ahead)
                        fz = tz[h, z, rows] * (v - v3[h, above, rows])
                        total = tx[h, z, rows] * (v - v3[h, z, up])
                        total = total + tx[h, z, down] * (v - v3[h, z, down])
                        v4[h, z, rows] = total + (ahead + back) + (fz - below[2 * n + h])
                        below[2 * n + h] = fz
            return tuple(below)

        lax.fori_loop(0, steps, block, (zero,) * (2 * len(OWN)))


    def exchange(value, slot, red, count, send, recv, where, meanwhile=None):
        send_row[slot:slot + 1, :] = value
        red[0:1, :] = value
        copies = []
        far = (lambda d: -min(d, count - d)) if count == gx else (
            lambda d: -min(d % 4, 4 - d % 4) - min(d // 4, 4 - d // 4))
        for d in sorted(range(1, count), key=far):
            copies.append(pltpu.make_async_remote_copy(
                src_ref=send_row.at[pl.ds(slot, 1), :],
                dst_ref=red.at[pl.ds(count - d, 1), :],
                send_sem=send.at[d],
                recv_sem=recv.at[count - d],
                device_id=where(d),
                device_id_type=MESH,
            ))
        for copy in copies:
            copy.start()
        if meanwhile is not None:
            meanwhile()
        for copy in copies:
            copy.wait_recv()
        return copies

    pl.semaphore_wait(barrier, gx - 1 + gy - 1)
    sent = exchange(row, 0, red_a, gx, a_send, a_recv, lambda d: (lax.rem(i + d, gx), j), fourth)
    part = red_a[...]
    hi, lo = tree(part, jnp.zeros_like(part))
    row = jnp.where(lane < 8, hi, pltpu.roll(lo, 8, 1))[0:1]
    sent += exchange(row, 8, red_b, gy, c_send, c_recv, lambda d: (i, lax.rem(j + d, gy)))
    parts = []
    for r in range(0, red_b.shape[0], 8):
        part = red_b[r:r + 8]
        parts.append((part, pltpu.roll(part, 120, 1)))
    total = parts[0]
    for part in parts[1:]:
        total = pair_add(total, part)
    hi, lo = tree(*total)
    splat = [
        (jnp.broadcast_to(hi[:, n:n + 1], (8, 128)), jnp.broadcast_to(lo[:, n:n + 1], (8, 128)))
        for n in range(8)
    ]
    for n, value in enumerate(coefficients(splat)):
        coef[n] = value

    for copy in sent:
        copy.wait_send()


def finish(nz, v0, v1, v2, v3, v4, tx, ty, q, coef, p_out, r_out, e_out, n_out,
           p_buf, r_buf, e_buf, n_buf, wide, side, sems):
    zp_count = nz // 8
    chunk = nz // PARTS
    lane = iota(1)
    c = [coef[n] for n in range(4)]

    def combine(parts):
        return (c[0] * parts[0] + c[1] * parts[1]) + (c[2] * parts[2] + c[3] * parts[3])

    for zp in range(zp_count):
        for r in OWN:
            side[zp, r:r + 8] = combine([q[k, zp, r:r + 8] for k in range(4)])

    def block(step, carry):
        moved = {}

        def first(u):
            z = BLOCK * step + u
            for r in OWN:
                press = []
                for h in range(2):
                    v = [f[h, z, r:r + 8] for f in (v0, v1, v2, v3)]
                    press.append(combine(v))
                    wide[u, h, r:r + 8] = press[h]
                    cols = slice(128 * h, 128 * h + 128)
                    p_buf[z, r - 8:r, cols] = press[h]
                    r_buf[z, r - 8:r, cols] = v[0] - combine(v[1:] + [v4[h, z, r:r + 8]])
                moved[u, r] = [roll(p, -1) for p in press]
                moved[u, r].append(edges(side, zp_count, step, u, r))
            for h in range(2):
                wide[u, h, 40:48] = combine([f[h, z, 40:48] for f in (v0, v1, v2, v3)])

        def second(u):
            z = BLOCK * step + u
            for r in OWN:
                one, two, rim = moved[u, r]
                for h, across in ((0, jnp.where(lane == 127, two, one)), (1, two)):
                    cols = slice(128 * h, 128 * h + 128)
                    press = wide[u, h, r:r + 8]
                    e_buf[z, r - 8:r, cols] = tx[h, z, r:r + 8] * (press - wide[u, h, r + 1:r + 9])
                    north = ty[h, z, r:r + 8] * (press - across)
                    if h == 1:
                        north = jnp.where(lane == 127, rim, north)
                    n_buf[z, r - 8:r, cols] = north

        for u in range(BLOCK):
            first(u)
            if u:
                second(u - 1)
        second(BLOCK - 1)
        return carry

    copies = []
    for part in range(PARTS):
        lax.fori_loop(part * chunk // BLOCK, (part + 1) * chunk // BLOCK, block, 0)
        for n, (buf, out) in enumerate(((p_buf, p_out), (r_buf, r_out), (e_buf, e_out), (n_buf, n_out))):
            copy = pltpu.make_async_copy(
                buf.at[pl.ds(part * chunk, chunk)],
                out.at[0, pl.ds(part * chunk, chunk)],
                sems.at[4 * part + n],
            )
            copy.start()
            copies.append(copy)
    for copy in copies:
        copy.wait()


def solution(mesh):
    gx, gy = mesh.shape["gx"], mesh.shape["gy"]

    def on_device(log_perm, source):
        nz = log_perm.shape[1]
        zp = nz // 8
        field = (2, nz, ROWS, 128)
        strip = (zp, ROWS, 128)
        vmem = pl.BlockSpec(memory_space=pltpu.VMEM)
        hbm = pl.BlockSpec(memory_space=pltpu.HBM)
        made = pl.pallas_call(
            functools.partial(gather, nz, gx, gy),
            out_shape=[pltpu.VMEM(field, F32)] * 7 + [pltpu.VMEM((5,) + strip, F32)],
            in_specs=[hbm] * 2,
            out_specs=[vmem] * 8,
            scratch_shapes=[pltpu.VMEM(field, F32)] * 2
            + [pltpu.VMEM(strip, F32)]
            + [pltpu.VMEM((zp // 2, ROWS, 128), F32)] * 4
            + [pltpu.VMEM(strip, F32)] * 9
            + [pltpu.SemaphoreType.DMA((4,))]
            + [pltpu.SemaphoreType.DMA((8,))] * 4,
            compiler_params=pltpu.CompilerParams(
                collective_id=0, has_side_effects=True, vmem_limit_bytes=16 << 20
            ),
            name="gather",
        )(*(pltpu.with_memory_space_constraint(x, pltpu.HBM) for x in (log_perm, source)))
        v0, tx, ty, tz, tym, yp, ym, q = made
        v1, v2, v3, v4, coef = pl.pallas_call(
            functools.partial(powers, nz, gx, gy),
            out_shape=[pltpu.VMEM(field, F32)] * 4 + [pltpu.VMEM((4, 8, 128), F32)],
            in_specs=[vmem] * 8,
            out_specs=[vmem] * 5,
            scratch_shapes=[pltpu.VMEM(field, F32)] * 4
            + [
                pltpu.VMEM((2, BLOCK, 5, 8, 128), F32),
                pltpu.VMEM((16, 128), F32),
                pltpu.VMEM((8, 128), F32),
                pltpu.VMEM((max(8, gy), 128), F32),
            ]
            + [pltpu.SemaphoreType.DMA((gx,))] * 2
            + [pltpu.SemaphoreType.DMA((gy,))] * 2,
            compiler_params=pltpu.CompilerParams(
                collective_id=1, has_side_effects=True, vmem_limit_bytes=14 << 20
            ),
            name="powers",
        )(*made)
        shape = jax.ShapeDtypeStruct(log_perm.shape, F32)
        return pl.pallas_call(
            functools.partial(finish, nz),
            out_shape=[shape] * 4,
            in_specs=[vmem] * 9,
            out_specs=[hbm] * 4,
            scratch_shapes=[pltpu.VMEM((nz, 32, 256), F32)] * 4
            + [pltpu.VMEM((BLOCK, 2, ROWS, 128), F32), pltpu.VMEM(strip, F32), pltpu.SemaphoreType.DMA((4 * PARTS,))],
            compiler_params=pltpu.CompilerParams(vmem_limit_bytes=12 << 20),
            name="finish",
        )(v0, v1, v2, v3, v4, tx, ty, q, coef)

    spec = P(None, None, "gx", "gy")
    return jax.shard_map(
        on_device, mesh=mesh, in_specs=(spec, spec), out_specs=(spec,) * 4, check_vma=False
    )
```
